512 devices in a mesh: row: 16 (over y, core), col: 32 (over z, x).
Axes of the slice: x: 4, y: 8, z: 8, core: 2. Of those that a mesh axis runs over, the one named last changes fastest.
Arguments:
- start_block: float32 [4, 65536], P(None, ('row', 'col')), may hold values from -6 to 6
- matrix_tiles: float32 [4096, 256, 256], P(('row', 'col')), may hold values from -0.125 to 0.125
- tile_rows: int32 [4096], P(('row', 'col')), may hold values from 0 to 255, as said below
- tile_cols: int32 [4096], P(('row', 'col')), may hold values from 0 to 255, as said below
- tile_counts: int32 [512], P(('row', 'col')), may hold values from 1 to 8
Outputs:
- next_basis: float32 [4, 65536], P(None, ('row', 'col'))
- next_residual: float32 [4, 65536], P(None, ('row', 'col'))
- coefficients: float32 [3, 4, 4], replicated
The draws below stay inside these ranges and needn't reach their ends.
Inputs may be any that keep to these rules, and one draw needn't show every extreme that they name: `tile_rows`: A slot of device d holds a tile whose row lies among the 16 tile rows (d // 32) * 16 onward and whose column lies among the 8 tile columns (d % 32) * 8 onward; its row I and column J satisfy I == J, or I < J with I + J odd, or I > J with I + J even; the slots of one device hold distinct tiles. `tile_cols`: paired with tile_rows slot by slot, as described there.
All inputs are finite; a program needn't handle non-finite values.
Results may differ from the reference program's by a relative error of at most 0.000098.
Values sent between devices are 32-bit elements; how exact they have to be, the bound alone decides.
A program may use at most 64 MiB of HBM per device.

```python
import jax
import jax.numpy as jnp
from jax import lax

TILE = 256
VEC = 4
SLOTS = 8
TBC = 8
TBR = 16
NT = 256
NDIM = 65536
DEVICES = 512


def tile_pattern(key):
    column_groups = NT // TBC
    region = TBR * TBC
    device_ids = jnp.arange(DEVICES, dtype=jnp.int32)[:, None]
    positions = jnp.arange(region, dtype=jnp.int32)[None, :]
    shuffled = jax.random.permutation(jax.random.fold_in(key, 7), jnp.broadcast_to(positions, (DEVICES, region)), axis=1, independent=True)
    row_tile = device_ids // column_groups * TBR + shuffled // TBC
    col_tile = device_ids % column_groups * TBC + shuffled % TBC
    parity = (row_tile + col_tile) % 2
    allowed = (row_tile == col_tile) | (row_tile < col_tile) & (parity == 1) | (row_tile > col_tile) & (parity == 0)
    ranking = jnp.where(allowed, 0, region) + positions
    chosen = jnp.argsort(ranking, axis=1)[:, :SLOTS]
    rows_out = jnp.take_along_axis(row_tile, chosen, axis=1).reshape(-1).astype(jnp.int32)
    cols_out = jnp.take_along_axis(col_tile, chosen, axis=1).reshape(-1).astype(jnp.int32)
    return (rows_out, cols_out)


def draw_tile_rows(key, part):
    return tile_pattern(key)[0]


def draw_tile_cols(key, part):
    return tile_pattern(key)[1]


def draw_tile_counts(key, part):
    lowest = max(1, 3 * SLOTS // 8)
    counted = jax.random.randint(jax.random.fold_in(key, 11), (DEVICES,), lowest, SLOTS + 1)
    return jnp.where(jnp.arange(DEVICES) == 0, SLOTS, counted).astype(jnp.int32)


def levels(rng, extent, cuts, low, largest):
    factor_of, own = 1.0, jax.random.fold_in(rng, 6)
    for axis_at, parts in cuts:
        heights = jnp.exp(jax.random.uniform(jax.random.fold_in(own, axis_at), (parts,), jnp.float32, low / len(cuts), largest / len(cuts)))
        factor_of = factor_of * jnp.repeat(heights, extent[axis_at] // parts).reshape([-1 if axis == axis_at else 1 for axis in range(len(extent))])
    return factor_of


def bell_draw(own_key, shape, spread, bound, shards=(), kind=jnp.bfloat16):
    gain = levels(own_key, shape, shards, -0.22, 0.18) if shards else 1.0
    values = jax.random.normal(own_key, shape, jnp.float32) * spread * gain
    return jnp.minimum(jnp.maximum(values, -bound), bound).astype(kind)


def setup_inputs(seed: int = 0) -> dict:
    keys = jax.random.split(jax.random.key(seed), 6)
    return {
        "start_block": bell_draw(keys[0], (VEC, NDIM), 1.0, 6.0, ((1, 512),), jnp.float32),
        "matrix_tiles": bell_draw(keys[1], (DEVICES * SLOTS, TILE, TILE), (8 * TILE) ** -0.5, 0.125, ((0, 512),), jnp.float32),
        "tile_rows": draw_tile_rows(jax.random.fold_in(keys[5], 71), 0),
        "tile_cols": draw_tile_cols(jax.random.fold_in(keys[5], 71), 0),
        "tile_counts": draw_tile_counts(jax.random.fold_in(keys[5], 71), 0),
    }


epsilon = 1e-06

def multiply(current, matrix_tiles, tile_rows, tile_cols, tile_counts):
    live_mask = (jnp.arange(matrix_tiles.shape[0], dtype=jnp.int32) % SLOTS < jnp.repeat(tile_counts, SLOTS)).astype(matrix_tiles.dtype)
    pieces = current.reshape(VEC, NT, TILE)
    from_cols = jnp.take(pieces, tile_cols, axis=1)
    from_rows = jnp.take(pieces, tile_rows, axis=1)
    forward = jnp.einsum('kab,ckb->kca', matrix_tiles, from_cols, precision=lax.Precision.HIGHEST) * live_mask[:, None, None]
    backward = jnp.einsum('kab,cka->kcb', matrix_tiles, from_rows, precision=lax.Precision.HIGHEST) * live_mask[:, None, None]
    summed = jax.ops.segment_sum(forward, tile_rows, NT) + jax.ops.segment_sum(backward, tile_cols, NT)
    return jnp.transpose(summed, (1, 0, 2)).reshape(VEC, NDIM)

def normalize(current):
    gram_matrix = jnp.dot(current, current.T, precision=lax.Precision.HIGHEST) / NDIM
    factor = jnp.linalg.cholesky(gram_matrix + epsilon * jnp.eye(VEC, dtype=gram_matrix.dtype))
    return (lax.linalg.triangular_solve(factor, current, left_side=True, lower=True), factor)

def reference(start_block, matrix_tiles, tile_rows, tile_cols, tile_counts):
    first_basis, start_factor = normalize(start_block)
    image = multiply(first_basis, matrix_tiles, tile_rows, tile_cols, tile_counts)
    first_diag = jnp.dot(first_basis, image.T, precision=lax.Precision.HIGHEST) / NDIM
    first_rest = image - jnp.dot(first_diag.T, first_basis, precision=lax.Precision.HIGHEST)
    next_basis, first_factor = normalize(first_rest)
    second_image = multiply(next_basis, matrix_tiles, tile_rows, tile_cols, tile_counts)
    second_diag = jnp.dot(next_basis, second_image.T, precision=lax.Precision.HIGHEST) / NDIM
    next_residual = second_image - jnp.dot(second_diag.T, next_basis, precision=lax.Precision.HIGHEST) - jnp.dot(first_factor.T, first_basis, precision=lax.Precision.HIGHEST)
    coefficients = jnp.stack([first_diag, second_diag, first_factor])
    return (next_basis, next_residual, coefficients)
```

```python
import jax
import jax.numpy as jnp
from jax import lax
from jax.experimental import pallas as pl
from jax.experimental.pallas import tpu as pltpu
from jax.sharding import PartitionSpec as P

MESH = pl.DeviceIdType.MESH
epsilon = 1e-06
VEC, TILE, SLOTS, LANES = 4, 256, 8, 128
ROWS, COLS = 16, 32
HALF = COLS // 2
ROW_TILES, COL_TILES = 16, 8
ORDER = ROWS * COLS * LANES

ROW0, COL0, FWD0, BWD0, ROW1, COL1, FWD1, BWD1, PLANE0, LINE0, PLANE1, LINE1, PLANE2, LINE2 = range(14)


def iota(shape, axis):
    return lax.broadcasted_iota(jnp.int32, shape, axis)


def apply(matrix, block):
    return sum(matrix[:, j : j + 1] * block[j : j + 1, :] for j in range(VEC))


def rotated(block, offset):
    if offset == 0:
        return block
    keep = iota((8, LANES), 0) % VEC + offset < VEC
    return jnp.where(keep, pltpu.roll(block, 8 - offset, 0), pltpu.roll(block, VEC - offset, 0))


def gram_row(products):
    total = jnp.zeros((8, LANES), jnp.float32)
    lane, row = iota((8, LANES), 1), iota((8, LANES), 0)
    for offset, product in enumerate(products):
        summed = jnp.sum(product, axis=1, keepdims=True)
        total = jnp.where(lane == VEC * offset + row % VEC, summed, total)
    return jnp.sum(total, axis=0, keepdims=True)


def entry(gram, base, i, j):
    lane = base + VEC * ((j - i) % VEC) + i
    return gram[:, lane : lane + 1]


def assemble(entries):
    lane, row = iota((VEC, LANES), 1), iota((VEC, LANES), 0)
    total = jnp.zeros((VEC, LANES), jnp.float32)
    for (i, j), value in entries.items():
        total = jnp.where((row == i) & (lane == j), value, total)
    return total


def factorize(gram, base):
    a = {(i, j): entry(gram, base, i, j) * (1.0 / ORDER) for i in range(VEC) for j in range(i + 1)}
    low, inv = {}, {}
    for j in range(VEC):
        pivot = a[j, j] + epsilon
        for k in range(j):
            pivot = pivot - low[j, k] * low[j, k]
        low[j, j] = jnp.sqrt(pivot)
        inv[j, j] = 1.0 / low[j, j]
        for i in range(j + 1, VEC):
            rest = a[i, j]
            for k in range(j):
                rest = rest - low[i, k] * low[j, k]
            low[i, j] = rest * inv[j, j]
    for j in range(VEC):
        for i in range(j + 1, VEC):
            rest = low[i, j] * inv[j, j]
            for k in range(j + 1, i):
                rest = rest + low[i, k] * inv[k, j]
            inv[i, j] = -rest * inv[i, i]
    flip = lambda entries: {(j, i): value for (i, j), value in entries.items()}
    return assemble(low), assemble(inv), assemble(flip(inv)), assemble(flip(low))


def projected(gram, inverse, inverse_t):
    entries = {}
    for i in range(VEC):
        for j in range(i + 1):
            value = (entry(gram, 0, i, j) + entry(gram, 0, j, i)) * (1.0 / ORDER)
            entries[i, j] = value
            entries[j, i] = value
    return apply(apply(inverse, assemble(entries)), inverse_t)


def split(block, row):
    high = block.astype(jnp.bfloat16).astype(jnp.float32)
    return jnp.where(row < VEC, high, block - high)


def twice(block):
    return jnp.concatenate([block, block], axis=0)


def kernel(
    x_ref, tiles_ref, rows_ref, cols_ref, count_ref,
    basis_ref, resid_ref, coef_ref,
    raw, t_high, t_low, own, xr, xc, row_parts, col_parts, row_packed,
    fp, bp, fr, br, gsrc, gp, gy, tsem, ssem, rsem,
):
    r, c = lax.axis_index("row"), lax.axis_index("col")
    group = 2 * r + c // HALF
    owner_row, owner_col = c // 2, HALF * (c % 2)
    lane_at = c % HALF
    eight = iota((8, LANES), 0)

    def send(src, dst, exchange, row, col):
        pltpu.make_async_remote_copy(
            src_ref=src, dst_ref=dst, send_sem=ssem.at[exchange], recv_sem=rsem.at[exchange],
            device_id=(row, col), device_id_type=MESH,
        ).start()

    def wait(sem, ref):
        pltpu.make_async_copy(ref, ref, sem).wait()

    def loop(first, last, body):
        def step(j, carry):
            body(j)
            return carry
        lax.fori_loop(first, last, step, 0)

    for k in range(SLOTS):
        pltpu.make_async_copy(tiles_ref.at[k], raw.at[k], tsem.at[k]).start()
    barrier = pltpu.get_barrier_semaphore()

    def greet(row, col):
        pl.semaphore_signal(barrier, 1, device_id=(row, col), device_id_type=MESH)

    loop(1, ROWS, lambda j: greet((r + j) % ROWS, group))

    @pl.when(owner_row != r)
    def _():
        loop(0, HALF, lambda j: greet(owner_row, owner_col + j))

    loop(1, COLS, lambda j: greet(r, (c + j) % COLS))

    def halve(k):
        wait(tsem.at[k], raw.at[k])
        tile = raw[k]
        high = tile.astype(jnp.bfloat16)
        t_high[k] = high
        t_low[k] = (tile - high.astype(jnp.float32)).astype(jnp.bfloat16)

    loop(0, SLOTS, halve)
    pl.semaphore_wait(barrier, jnp.where(owner_row != r, COLS - 1 + ROWS - 1 + HALF, COLS - 1 + ROWS - 1))

    def gather(step, src, row_exchange, col_exchange):
        dst = xc.at[step, lane_at]
        loop(1, ROWS, lambda j: send(src, dst, col_exchange, (r + j) % ROWS, group))

        @pl.when(group == c)
        def _():
            pltpu.make_async_copy(src, dst, rsem.at[col_exchange]).start()

        @pl.when(group != c)
        def _():
            send(src, dst, col_exchange, r, group)

        loop(1, COLS, lambda j: send(src, xr.at[step, c], row_exchange, r, (c + j) % COLS))
        xr[step, c] = src[...]

    def gathered(step, row_exchange, col_exchange):
        wait(rsem.at[row_exchange], xr.at[step, pl.ds(0, COLS - 1)])
        wait(rsem.at[col_exchange], xc.at[step])

    def scatter(step, fwd_exchange, bwd_exchange):
        dst = br.at[step, r]

        def one(j):
            s = (c + j) % HALF
            send(bp.at[step, s], dst, bwd_exchange, owner_row, owner_col + s)

        loop(1, HALF, one)
        mine = (owner_row == r) & (owner_col + lane_at == c)

        @pl.when(mine)
        def _():
            pltpu.make_async_copy(bp.at[step, lane_at], dst, rsem.at[bwd_exchange]).start()

        @pl.when(jnp.logical_not(mine))
        def _():
            one(0)

        def two(j):
            p = (c + j) % COLS
            send(fp.at[step, p], fr.at[step, c], fwd_exchange, r, p)

        loop(1, COLS, two)
        fr[step, c] = fp[step, c]

    def scattered(step, fwd_exchange, bwd_exchange):
        wait(rsem.at[fwd_exchange], fr.at[step, pl.ds(0, COLS - 1)])
        wait(rsem.at[bwd_exchange], br.at[step])
        return jnp.sum(fr[step], axis=0) + jnp.sum(br[step], axis=0)

    def plane_start(at, value, exchange):
        gsrc[2 * at] = value
        gp[at, c] = value
        loop(1, COLS, lambda j: send(gsrc.at[2 * at], gp.at[at, c], exchange, r, (c + j) % COLS))

    def line_start(at, plane_exchange, line_exchange):
        wait(rsem.at[plane_exchange], gp.at[at, pl.ds(0, COLS - 1)])
        value = jnp.sum(gp[at], axis=0)
        gsrc[2 * at + 1] = value
        gy[at, r] = value
        loop(1, ROWS, lambda j: send(gsrc.at[2 * at + 1], gy.at[at, r], line_exchange, (r + j) % ROWS, c))

    def line_done(at, line_exchange):
        wait(rsem.at[line_exchange], gy.at[at, pl.ds(0, ROWS - 1)])
        return jnp.sum(gy[at], axis=0)

    def products(step):
        live = count_ref[0]
        forward, backward, row_at, col_at = [], [], [], []
        cross = [jnp.zeros((8, LANES), jnp.float32) for _ in range(VEC)]
        for k in range(SLOTS):
            i, j = rows_ref[k] & (ROW_TILES - 1), cols_ref[k] & (COL_TILES - 1)
            mask = jnp.where(k < live, 1.0, 0.0).astype(jnp.float32)
            from_col, from_row = col_parts[pl.ds(2 * j, 2)], row_parts[pl.ds(2 * i, 2)]
            from_col = jnp.concatenate([from_col[0], from_col[1]], axis=1).astype(jnp.bfloat16)
            from_row = jnp.concatenate([from_row[0], from_row[1]], axis=1).astype(jnp.bfloat16)

            def multiply(block, dims):
                high = lax.dot_general(block, t_high[k], (dims, ((), ())), preferred_element_type=jnp.float32)
                low = lax.dot_general(block, t_low[k], (dims, ((), ())), preferred_element_type=jnp.float32)
                both = high + low
                left, right = both[:, :LANES], both[:, LANES:]
                left = left + pltpu.roll(left, VEC, 0)
                right = right + pltpu.roll(right, VEC, 0)
                return jnp.where(eight < VEC, left, right) * mask

            ahead = multiply(from_col, ((1,), (1,)))
            forward.append(ahead)
            backward.append(multiply(from_row, ((1,), (0,))))
            row_at.append(i)
            col_at.append(j)
            entries = row_packed[i]
            for offset in range(VEC):
                cross[offset] = cross[offset] + entries * rotated(ahead, offset)
        for values, places, out, tiles in ((backward, col_at, bp, COL_TILES), (forward, row_at, fp, ROW_TILES)):
            for t in range(tiles):
                total = jnp.where(places[0] == t, values[0], 0.0)
                for k in range(1, SLOTS):
                    total = total + jnp.where(places[k] == t, values[k], 0.0)
                out[step, 2 * t] = total[:VEC]
                out[step, 2 * t + 1] = total[VEC:]
        return cross

    gather(0, x_ref, ROW0, COL0)
    start = x_ref[...]
    start_twice = twice(start)
    half = jnp.where(eight < VEC, start_twice, 0.0)
    start_row = gram_row([half * rotated(start_twice, offset) for offset in range(VEC)])
    gathered(0, ROW0, COL0)
    for t in range(ROW_TILES):
        left, right = twice(xr[0, 2 * t]), twice(xr[0, 2 * t + 1])
        row_parts[2 * t] = split(left, eight)
        row_parts[2 * t + 1] = split(right, eight)
        row_packed[t] = jnp.where(eight < VEC, left, right)
    for s in range(HALF):
        col_parts[s] = split(twice(xc[0, s]), eight)
    cross = products(0)
    scatter(0, FWD0, BWD0)
    plane_start(0, gram_row(cross) + pltpu.roll(start_row, 16, 1), PLANE0)
    line_start(0, PLANE0, LINE0)
    image = scattered(0, FWD0, BWD0)
    own[...] = image

    gather(1, own, ROW1, COL1)
    gram = line_done(0, LINE0)
    _, inverse, inverse_t, _ = factorize(gram, 16)
    first_diag = projected(gram, inverse, inverse_t)
    first_basis = apply(inverse, start)
    from_start = -apply(first_diag, inverse)
    rest = apply(inverse, image) + apply(from_start, start)
    rest_twice = twice(rest)
    half = jnp.where(eight < VEC, rest_twice, 0.0)
    plane_start(1, gram_row([half * rotated(rest_twice, offset) for offset in range(VEC)]), PLANE1)
    inverse_twice, start_factor_twice = twice(inverse), twice(from_start)
    of_image = [jnp.broadcast_to(inverse_twice[:, j : j + 1], (8, LANES)) for j in range(VEC)]
    of_start = [jnp.broadcast_to(start_factor_twice[:, j : j + 1], (8, LANES)) for j in range(VEC)]

    def combined(ref, at):
        total = of_image[0] * ref[1, at, 0:1, :] + of_start[0] * ref[0, at, 0:1, :]
        for j in range(1, VEC):
            total = total + (of_image[j] * ref[1, at, j : j + 1, :] + of_start[j] * ref[0, at, j : j + 1, :])
        return total

    gathered(1, ROW1, COL1)
    for t in range(ROW_TILES):
        left, right = combined(xr, 2 * t), combined(xr, 2 * t + 1)
        row_parts[2 * t] = split(left, eight)
        row_parts[2 * t + 1] = split(right, eight)
        row_packed[t] = jnp.where(eight < VEC, left, right)
    for s in range(HALF):
        col_parts[s] = split(combined(xc, s), eight)
    cross = products(1)
    scatter(1, FWD1, BWD1)
    plane_start(2, gram_row(cross), PLANE2)
    line_start(1, PLANE1, LINE1)
    line_start(2, PLANE2, LINE2)
    gram = line_done(1, LINE1)
    factor, inverse, inverse_t, factor_t = factorize(gram, 0)
    next_basis = apply(inverse, rest)
    basis_ref[...] = next_basis
    image = scattered(1, FWD1, BWD1)
    known = apply(inverse, image) - apply(factor_t, first_basis)
    gram = line_done(2, LINE2)
    second_diag = projected(gram, inverse, inverse_t)
    resid_ref[...] = known - apply(second_diag, next_basis)
    coef_ref[0] = first_diag[:, :VEC]
    coef_ref[1] = second_diag[:, :VEC]
    coef_ref[2] = factor[:, :VEC]

    for step, row_exchange, col_exchange, fwd_exchange, bwd_exchange in (
        (0, ROW0, COL0, FWD0, BWD0), (1, ROW1, COL1, FWD1, BWD1)
    ):
        wait(ssem.at[row_exchange], xr.at[step, pl.ds(0, COLS - 1)])
        wait(ssem.at[fwd_exchange], fr.at[step, pl.ds(0, COLS - 1)])

        wait(ssem.at[col_exchange], xc.at[step, pl.ds(0, ROWS - 1)])

        @pl.when(group != c)
        def _():
            wait(ssem.at[col_exchange], xc.at[step, 0])

        wait(ssem.at[bwd_exchange], br.at[step, pl.ds(0, HALF - 1)])

        @pl.when(jnp.logical_not((owner_row == r) & (owner_col + lane_at == c)))
        def _():
            wait(ssem.at[bwd_exchange], br.at[step, 0])

    for at, plane_exchange, line_exchange in ((0, PLANE0, LINE0), (1, PLANE1, LINE1), (2, PLANE2, LINE2)):
        wait(ssem.at[plane_exchange], gp.at[at, pl.ds(0, COLS - 1)])
        wait(ssem.at[line_exchange], gy.at[at, pl.ds(0, ROWS - 1)])


def body(start_block, matrix_tiles, tile_rows, tile_cols, tile_counts):
    share = jax.ShapeDtypeStruct((VEC, LANES), jnp.float32)
    vmem, smem = pl.BlockSpec(memory_space=pltpu.VMEM), pl.BlockSpec(memory_space=pltpu.SMEM)
    buffer = lambda *shape: pltpu.VMEM(shape, jnp.float32)
    return pl.pallas_call(
        kernel,
        out_shape=(share, share, jax.ShapeDtypeStruct((3, VEC, VEC), jnp.float32)),
        in_specs=[vmem, pl.BlockSpec(memory_space=pl.ANY), smem, smem, smem],
        out_specs=(vmem, vmem, vmem),
        scratch_shapes=[
            buffer(SLOTS, TILE, TILE),
            pltpu.VMEM((SLOTS, TILE, TILE), jnp.bfloat16),
            pltpu.VMEM((SLOTS, TILE, TILE), jnp.bfloat16),
            buffer(VEC, LANES),
            buffer(2, COLS, VEC, LANES),
            buffer(2, HALF, VEC, LANES),
            buffer(COLS, 8, LANES),
            buffer(HALF, 8, LANES),
            buffer(ROW_TILES, 8, LANES),
            buffer(2, COLS, VEC, LANES),
            buffer(2, HALF, VEC, LANES),
            buffer(2, COLS, VEC, LANES),
            buffer(2, ROWS, VEC, LANES),
            buffer(6, 1, LANES),
            buffer(3, COLS, 1, LANES),
            buffer(3, ROWS, 1, LANES),
            pltpu.SemaphoreType.DMA((SLOTS,)),
            pltpu.SemaphoreType.DMA((14,)),
            pltpu.SemaphoreType.DMA((14,)),
        ],
        compiler_params=pltpu.CompilerParams(collective_id=0, has_side_effects=True),
    )(start_block, matrix_tiles, tile_rows, tile_cols, tile_counts)


def solution(mesh):
    return jax.shard_map(
        body,
        mesh=mesh,
        in_specs=(
            P(None, ("row", "col")),
            P(("row", "col"), None, None),
            P(("row", "col")),
            P(("row", "col")),
            P(("row", "col")),
        ),
        out_specs=(P(None, ("row", "col")), P(None, ("row", "col")), P()),
        check_vma=False,
    )
```

```python
import jax
import jax.numpy as jnp
from jax import lax
from jax.experimental import pallas as pl
from jax.experimental.pallas import tpu as pltpu
from jax.sharding import PartitionSpec as P

MESH = pl.DeviceIdType.MESH
epsilon = 1e-06
VEC, TILE, SLOTS, LANES = 4, 256, 8, 128
ROWS, COLS = 16, 32
HALF = COLS // 2
ROW_TILES, COL_TILES = 16, 8
ORDER = ROWS * COLS * LANES

ROW0, COL0, FWD0, BWD0, ROW1, COL1, FWD1, BWD1, PLANE0, LINE0, PLANE1, LINE1, PLANE2, LINE2 = range(14)


def iota(shape, axis):
    return lax.broadcasted_iota(jnp.int32, shape, axis)


def apply(matrix, block):
    return sum(matrix[:, j : j + 1] * block[j : j + 1, :] for j in range(VEC))


def rotated(block, offset):
    if offset == 0:
        return block
    keep = iota((8, LANES), 0) % VEC + offset < VEC
    return jnp.where(keep, pltpu.roll(block, 8 - offset, 0), pltpu.roll(block, VEC - offset, 0))


def gram_row(products):
    total = jnp.zeros((8, LANES), jnp.float32)
    lane, row = iota((8, LANES), 1), iota((8, LANES), 0)
    for offset, product in enumerate(products):
        summed = jnp.sum(product, axis=1, keepdims=True)
        total = jnp.where(lane == VEC * offset + row % VEC, summed, total)
    return jnp.sum(total, axis=0, keepdims=True)


def entry(gram, base, i, j):
    lane = base + VEC * ((j - i) % VEC) + i
    return gram[:, lane : lane + 1]


def assemble(entries):
    lane, row = iota((VEC, LANES), 1), iota((VEC, LANES), 0)
    total = jnp.zeros((VEC, LANES), jnp.float32)
    for (i, j), value in entries.items():
        total = jnp.where((row == i) & (lane == j), value, total)
    return total


def factorize(gram, base):
    a = {(i, j): entry(gram, base, i, j) * (1.0 / ORDER) for i in range(VEC) for j in range(i + 1)}
    low, inv = {}, {}
    for j in range(VEC):
        pivot = a[j, j] + epsilon
        for k in range(j):
            pivot = pivot - low[j, k] * low[j, k]
        low[j, j] = jnp.sqrt(pivot)
        inv[j, j] = 1.0 / low[j, j]
        for i in range(j + 1, VEC):
            rest = a[i, j]
            for k in range(j):
                rest = rest - low[i, k] * low[j, k]
            low[i, j] = rest * inv[j, j]
    for j in range(VEC):
        for i in range(j + 1, VEC):
            rest = low[i, j] * inv[j, j]
            for k in range(j + 1, i):
                rest = rest + low[i, k] * inv[k, j]
            inv[i, j] = -rest * inv[i, i]
    flip = lambda entries: {(j, i): value for (i, j), value in entries.items()}
    return assemble(low), assemble(inv), assemble(flip(inv)), assemble(flip(low))


def projected(gram, inverse, inverse_t):
    entries = {}
    for i in range(VEC):
        for j in range(i + 1):
            value = (entry(gram, 0, i, j) + entry(gram, 0, j, i)) * (1.0 / ORDER)
            entries[i, j] = value
            entries[j, i] = value
    return apply(apply(inverse, assemble(entries)), inverse_t)


def split(block, row):
    high = block.astype(jnp.bfloat16).astype(jnp.float32)
    return jnp.where(row < VEC, high, block - high)


def twice(block):
    return jnp.concatenate([block, block], axis=0)


def kernel(
    x_hbm, tiles_hbm, rows_hbm, cols_hbm, count_hbm,
    basis_ref, resid_ref, coef_ref,
    x_ref, rows_ref, cols_ref, count_ref, raw, t_high, t_low, own, xr, xc, row_parts, col_parts, row_packed,
    fp, bp, fr, br, fm, bm, gsrc, gy, gp, isem, tsem, ssem, rsem,
):
    r, c = lax.axis_index("row"), lax.axis_index("col")
    y, core, z, x = lax.div(r, 2), lax.rem(r, 2), lax.div(c, 4), lax.rem(c, 4)
    group = 2 * r + lax.div(c, HALF)
    owner_row, owner_col = lax.div(c, 2), HALF * lax.rem(c, 2)
    lane_at = lax.rem(c, HALF)
    eight = iota((8, LANES), 0)

    turn = lax.rem(x + 4 - 2 * core, 4)
    odd = jnp.where((turn == 1) | (turn == 2), 1, 0)
    near = lax.rem(z + 9 - y, 8)
    keeper = near < 4
    kept_pair = jnp.where(keeper, near, 0) + jnp.where(turn >= 2, 4, 0)
    kept_group = 2 * r + odd

    def keeper_col(g, q):
        at_z = lax.rem(lax.div(g, 4) + 7 + lax.rem(q, 4), 8)
        at_x = lax.rem(g + 4 + (2 * lax.rem(g, 2) - 1) * lax.div(q, 4), 4)
        return 4 * at_z + at_x

    def send(src, dst, exchange, row, col):
        pltpu.make_async_remote_copy(
            src_ref=src, dst_ref=dst, send_sem=ssem.at[exchange], recv_sem=rsem.at[exchange],
            device_id=(row, col), device_id_type=MESH,
        ).start()

    def send_or_keep(src, dst, exchange, row, col):
        mine = (row == r) & (col == c)

        @pl.when(mine)
        def _():
            pltpu.make_async_copy(src, dst, rsem.at[exchange]).start()

        @pl.when(jnp.logical_not(mine))
        def _():
            send(src, dst, exchange, row, col)

    def wait(sem, ref):
        pltpu.make_async_copy(ref, ref, sem).wait()

    def loop(first, last, body):
        def step(j, carry):
            body(j)
            return carry
        lax.fori_loop(first, last, step, 0)

    pending = []

    pltpu.make_async_copy(x_hbm, x_ref, isem.at[0]).start()
    barrier = pltpu.get_barrier_semaphore()

    def greet(row, col):
        pl.semaphore_signal(barrier, 1, device_id=(row, col), device_id_type=MESH)

    loop(1, ROWS, lambda j: greet(lax.rem(r + j, ROWS), group))

    @pl.when(owner_row != r)
    def _():
        loop(0, HALF, lambda j: greet(owner_row, owner_col + j))

    loop(1, COLS, lambda j: greet(r, lax.rem(c + j, COLS)))
    for k in range(SLOTS):
        pltpu.make_async_copy(tiles_hbm.at[k], raw.at[k], tsem.at[k]).start()
    pltpu.make_async_copy(rows_hbm, rows_ref, isem.at[1]).start()
    pltpu.make_async_copy(cols_hbm, cols_ref, isem.at[2]).start()
    pltpu.make_async_copy(count_hbm, count_ref, isem.at[3]).start()
    wait(isem.at[0], x_ref)
    pl.semaphore_wait(barrier, jnp.where(owner_row != r, COLS - 1 + ROWS - 1 + HALF, COLS - 1 + ROWS - 1))

    def line_start(at, value, exchange):
        gsrc[2 * at] = value
        gy[at, r] = value
        loop(1, ROWS, lambda j: send(gsrc.at[2 * at], gy.at[at, r], exchange, lax.rem(r + j, ROWS), c))
        pending.append((exchange, gy.at[at, pl.ds(0, ROWS - 1)], None))

    def plane_start(at, line_exchange, exchange):
        wait(rsem.at[line_exchange], gy.at[at, pl.ds(0, ROWS - 1)])
        value = jnp.sum(gy[at], axis=0)
        gsrc[2 * at + 1] = value
        gp[at, c] = value
        loop(1, COLS, lambda j: send(gsrc.at[2 * at + 1], gp.at[at, c], exchange, r, lax.rem(c + j, COLS)))
        pending.append((exchange, gp.at[at, pl.ds(0, COLS - 1)], None))

    def plane_done(at, exchange):
        wait(rsem.at[exchange], gp.at[at, pl.ds(0, COLS - 1)])
        return jnp.sum(gp[at], axis=0)

    def spread(step, values, places, out, tiles):
        for t in range(tiles):
            total = jnp.where(places[0] == t, values[0], 0.0)
            for k in range(1, SLOTS):
                total = total + jnp.where(places[k] == t, values[k], 0.0)
            out[step, 2 * t] = total[:VEC]
            out[step, 2 * t + 1] = total[VEC:]

    def places():
        row_at = [lax.rem(rows_ref[k], ROW_TILES) for k in range(SLOTS)]
        col_at = [lax.rem(cols_ref[k], COL_TILES) for k in range(SLOTS)]
        masks = [jnp.where(k < count_ref[0], 1.0, 0.0).astype(jnp.float32) for k in range(SLOTS)]
        return row_at, col_at, masks

    def multiply(k, parts, at, dims, mask):
        block = parts[pl.ds(2 * at, 2)]
        block = jnp.concatenate([block[0], block[1]], axis=1).astype(jnp.bfloat16)
        high = lax.dot_general(block, t_high[k], (dims, ((), ())), preferred_element_type=jnp.float32)
        low = lax.dot_general(block, t_low[k], (dims, ((), ())), preferred_element_type=jnp.float32)
        both = high + low
        left, right = both[:, :LANES], both[:, LANES:]
        left = left + pltpu.roll(left, VEC, 0)
        right = right + pltpu.roll(right, VEC, 0)
        return jnp.where(eight < VEC, left, right) * mask

    def crossed(forward, row_at):
        cross = [jnp.zeros((8, LANES), jnp.float32) for _ in range(VEC)]
        for k in range(SLOTS):
            entries = row_packed[row_at[k]]
            for offset in range(VEC):
                cross[offset] = cross[offset] + entries * rotated(forward[k], offset)
        return gram_row(cross)

    def own_gram(block):
        block = twice(block)
        half = jnp.where(eight < VEC, block, 0.0)
        return gram_row([half * rotated(block, offset) for offset in range(VEC)])

    dst = xc.at[0, lane_at]
    loop(1, ROWS, lambda j: send(x_ref, dst, COL0, lax.rem(r + j, ROWS), group))
    send_or_keep(x_ref, dst, COL0, r, group)
    loop(1, COLS, lambda j: send(x_ref, xr.at[0, c], ROW0, r, lax.rem(c + j, COLS)))
    start = x_ref[...]
    xr[0, c] = start
    pending.append((ROW0, xr.at[0, pl.ds(0, COLS - 1)], None))
    pending.append((COL0, xc.at[0, pl.ds(0, ROWS - 1)], None))
    pending.append((COL0, xc.at[0, 0], group != c))

    def halve(k):
        wait(tsem.at[k], raw.at[k])
        tile = raw[k]
        high = tile.astype(jnp.bfloat16)
        t_high[k] = high
        t_low[k] = (tile - high.astype(jnp.float32)).astype(jnp.bfloat16)

    loop(0, SLOTS, halve)
    wait(isem.at[1], rows_ref)
    wait(isem.at[2], cols_ref)
    wait(isem.at[3], count_ref)
    row_at, col_at, masks = places()
    start_row = pltpu.roll(own_gram(start), 16, 1)
    wait(rsem.at[ROW0], xr.at[0, pl.ds(0, COLS - 1)])
    for t in range(ROW_TILES):
        left, right = twice(xr[0, 2 * t]), twice(xr[0, 2 * t + 1])
        row_parts[2 * t] = split(left, eight)
        row_parts[2 * t + 1] = split(right, eight)
        row_packed[t] = jnp.where(eight < VEC, left, right)
    wait(rsem.at[COL0], xc.at[0])
    for s in range(HALF):
        col_parts[s] = split(twice(xc[0, s]), eight)
    backward = [multiply(k, row_parts, row_at[k], ((1,), (0,)), masks[k]) for k in range(SLOTS)]
    spread(0, backward, col_at, bp, COL_TILES)

    loop(0, 8, lambda q: send_or_keep(bp.at[0, pl.ds(2 * q, 2)], bm.at[r], BWD0, owner_row, keeper_col(c, q)))
    forward = [multiply(k, col_parts, col_at[k], ((1,), (1,)), masks[k]) for k in range(SLOTS)]
    spread(0, forward, row_at, fp, ROW_TILES)
    loop(0, HALF, lambda q: send_or_keep(
        fp.at[0, pl.ds(2 * q, 2)], fm.at[c], FWD0, r, keeper_col(2 * r + lax.div(q, 8), lax.rem(q, 8))))
    pending.append((BWD0, bp.at[0, pl.ds(0, HALF - 2)], None))
    pending.append((BWD0, bp.at[0, pl.ds(0, 2)], jnp.logical_not(keeper & (kept_group == c))))
    pending.append((FWD0, fp.at[0, pl.ds(0, COLS - 2)], None))
    pending.append((FWD0, fp.at[0, pl.ds(0, 2)], jnp.logical_not(keeper)))
    line_start(0, crossed(forward, row_at) + start_row, LINE0)

    at_row = xr.at[1, pl.ds(HALF * odd + 2 * kept_pair, 2)]
    at_col = xc.at[1, pl.ds(2 * kept_pair, 2)]

    @pl.when(keeper)
    def _():
        wait(rsem.at[FWD0], fm)
        ahead = jnp.sum(fm[...], axis=0)
        wait(rsem.at[BWD0], bm)
        own[...] = ahead + jnp.sum(bm[...], axis=0)
        loop(0, ROWS, lambda j: send_or_keep(own, at_col, COL1, lax.rem(r + j, ROWS), kept_group))
        loop(1, COLS, lambda j: send(own, at_row, ROW1, r, lax.rem(c + j, COLS)))
        pltpu.make_async_copy(own, at_row, rsem.at[ROW1]).start()

    for lap in range(2):
        pending.append((ROW1, xr.at[1, pl.ds(0, COLS - 1)], keeper))
    pending.append((COL1, xc.at[1, pl.ds(0, HALF)], keeper))
    pending.append((COL1, xc.at[1, pl.ds(0, HALF - 2)], keeper))
    pending.append((COL1, xc.at[1, pl.ds(0, 2)], keeper & (kept_group != c)))

    plane_start(0, LINE0, PLANE0)
    gram = plane_done(0, PLANE0)
    _, inverse, inverse_t, _ = factorize(gram, 16)
    first_diag = projected(gram, inverse, inverse_t)
    first_basis = apply(inverse, start)
    from_start = -apply(first_diag, inverse)
    inverse_twice, start_factor_twice = twice(inverse), twice(from_start)
    of_image = [jnp.broadcast_to(inverse_twice[:, j : j + 1], (8, LANES)) for j in range(VEC)]
    of_start = [jnp.broadcast_to(start_factor_twice[:, j : j + 1], (8, LANES)) for j in range(VEC)]

    def combined(ref, at):
        total = of_image[0] * ref[1, at, 0:1, :] + of_start[0] * ref[0, at, 0:1, :]
        for j in range(1, VEC):
            total = total + (of_image[j] * ref[1, at, j : j + 1, :] + of_start[j] * ref[0, at, j : j + 1, :])
        return total

    wait(rsem.at[ROW1], xr.at[1])
    rest = apply(inverse, xr[1, c]) + apply(from_start, start)
    rest_row = own_gram(rest)
    line_start(1, rest_row, LINE1)
    for t in range(ROW_TILES):
        left, right = combined(xr, 2 * t), combined(xr, 2 * t + 1)
        row_parts[2 * t] = split(left, eight)
        row_parts[2 * t + 1] = split(right, eight)
        row_packed[t] = jnp.where(eight < VEC, left, right)
    wait(rsem.at[COL1], xc.at[1])
    for s in range(HALF):
        col_parts[s] = split(combined(xc, s), eight)
    forward = [multiply(k, col_parts, col_at[k], ((1,), (1,)), masks[k]) for k in range(SLOTS)]
    line_start(2, crossed(forward, row_at), LINE2)
    backward = [multiply(k, row_parts, row_at[k], ((1,), (0,)), masks[k]) for k in range(SLOTS)]
    spread(1, backward, col_at, bp, COL_TILES)

    def back(j):
        s = lax.rem(c + j, HALF)
        send_or_keep(bp.at[1, s], br.at[r], BWD1, owner_row, owner_col + s)

    loop(0, HALF, back)
    spread(1, forward, row_at, fp, ROW_TILES)

    def ahead(j):
        p = lax.rem(c + j, COLS)
        send(fp.at[1, p], fr.at[c], FWD1, r, p)

    loop(1, COLS, ahead)
    fr[c] = fp[1, c]
    pending.append((FWD1, fr.at[pl.ds(0, COLS - 1)], None))
    pending.append((BWD1, br.at[pl.ds(0, HALF - 1)], None))
    pending.append((BWD1, br.at[0], group != c))
    plane_start(1, LINE1, PLANE1)
    plane_start(2, LINE2, PLANE2)
    gram = plane_done(1, PLANE1)
    factor, inverse, inverse_t, factor_t = factorize(gram, 0)
    next_basis = apply(inverse, rest)
    basis_ref[...] = next_basis
    wait(rsem.at[FWD1], fr.at[pl.ds(0, COLS - 1)])
    image = jnp.sum(fr[...], axis=0)
    wait(rsem.at[BWD1], br)
    image = image + jnp.sum(br[...], axis=0)
    known = apply(inverse, image) - apply(factor_t, first_basis)
    for exchange, ref, condition in pending[:-1]:
        if condition is None:
            wait(ssem.at[exchange], ref)
        else:
            pl.when(condition)(lambda exchange=exchange, ref=ref: wait(ssem.at[exchange], ref))
    gram = plane_done(2, PLANE2)
    second_diag = projected(gram, inverse, inverse_t)
    resid_ref[...] = known - apply(second_diag, next_basis)
    coef_ref[0] = first_diag[:, :VEC]
    coef_ref[1] = second_diag[:, :VEC]
    coef_ref[2] = factor[:, :VEC]
    wait(ssem.at[pending[-1][0]], pending[-1][1])


def settle(basis, resid, coef, basis_out, resid_out, coef_out, sem):
    copies = [
        pltpu.make_async_copy(src, dst, sem.at[at])
        for at, (src, dst) in enumerate(((basis, basis_out), (resid, resid_out), (coef, coef_out)))
    ]
    for copy in copies:
        copy.start()
    for copy in copies:
        copy.wait()


def body(start_block, matrix_tiles, tile_rows, tile_cols, tile_counts):
    share = jax.ShapeDtypeStruct((VEC, LANES), jnp.float32)
    shapes = (share, share, jax.ShapeDtypeStruct((3, VEC, VEC), jnp.float32))
    vmem, anywhere = pl.BlockSpec(memory_space=pltpu.VMEM), pl.BlockSpec(memory_space=pl.ANY)
    buffer = lambda *shape: pltpu.VMEM(shape, jnp.float32)
    found = pl.pallas_call(
        kernel,
        out_shape=shapes,
        in_specs=[anywhere] * 5,
        out_specs=(vmem, vmem, vmem),
        scratch_shapes=[
            buffer(VEC, LANES),
            pltpu.SMEM((SLOTS,), jnp.int32),
            pltpu.SMEM((SLOTS,), jnp.int32),
            pltpu.SMEM((1,), jnp.int32),
            buffer(SLOTS, TILE, TILE),
            pltpu.VMEM((SLOTS, TILE, TILE), jnp.bfloat16),
            pltpu.VMEM((SLOTS, TILE, TILE), jnp.bfloat16),
            buffer(2, VEC, LANES),
            buffer(2, COLS, VEC, LANES),
            buffer(2, HALF, VEC, LANES),
            buffer(COLS, 8, LANES),
            buffer(HALF, 8, LANES),
            buffer(ROW_TILES, 8, LANES),
            buffer(2, COLS, VEC, LANES),
            buffer(2, HALF, VEC, LANES),
            buffer(COLS, VEC, LANES),
            buffer(ROWS, VEC, LANES),
            buffer(COLS, 2, VEC, LANES),
            buffer(ROWS, 2, VEC, LANES),
            buffer(6, 1, LANES),
            buffer(3, ROWS, 1, LANES),
            buffer(3, COLS, 1, LANES),
            pltpu.SemaphoreType.DMA((4,)),
            pltpu.SemaphoreType.DMA((SLOTS,)),
            pltpu.SemaphoreType.DMA((14,)),
            pltpu.SemaphoreType.DMA((14,)),
        ],
        compiler_params=pltpu.CompilerParams(collective_id=0, has_side_effects=True),
    )(start_block, matrix_tiles, tile_rows, tile_cols, tile_counts)
    return pl.pallas_call(
        settle,
        out_shape=shapes,
        in_specs=[anywhere] * 3,
        out_specs=(anywhere, anywhere, anywhere),
        scratch_shapes=[pltpu.SemaphoreType.DMA((3,))],
    )(*found)


def solution(mesh):
    return jax.shard_map(
        body,
        mesh=mesh,
        in_specs=(
            P(None, ("row", "col")),
            P(("row", "col"), None, None),
            P(("row", "col")),
            P(("row", "col")),
            P(("row", "col")),
        ),
        out_specs=(P(None, ("row", "col")), P(None, ("row", "col")), P()),
        check_vma=False,
    )
```

```python
import jax
import jax.numpy as jnp
from jax import lax
from jax.experimental import pallas as pl
from jax.experimental.pallas import tpu as pltpu
from jax.sharding import PartitionSpec as P

MESH = pl.DeviceIdType.MESH
epsilon = 1e-06
VEC, TILE, SLOTS, LANES = 4, 256, 8, 128
ROWS, COLS = 16, 32
HALF = COLS // 2
ROW_TILES, COL_TILES = 16, 8
ORDER = ROWS * COLS * LANES

ROW0, COL0, FWD0, BWD0, ROW1, COL1, FWD1, BWD1, PLANE0, LINE0, PLANE1, LINE1, PLANE2, LINE2 = range(14)


def iota(shape, axis):
    return lax.broadcasted_iota(jnp.int32, shape, axis)


def apply(matrix, block):
    return sum(matrix[:, j : j + 1] * block[j : j + 1, :] for j in range(VEC))


def rotated(block, offset):
    if offset == 0:
        return block
    keep = iota((8, LANES), 0) % VEC + offset < VEC
    return jnp.where(keep, pltpu.roll(block, 8 - offset, 0), pltpu.roll(block, VEC - offset, 0))


def gram_row(products):
    total = jnp.zeros((8, LANES), jnp.float32)
    lane, row = iota((8, LANES), 1), iota((8, LANES), 0)
    for offset, product in enumerate(products):
        summed = jnp.sum(product, axis=1, keepdims=True)
        total = jnp.where(lane == VEC * offset + row % VEC, summed, total)
    return jnp.sum(total, axis=0, keepdims=True)


def entry(gram, base, i, j):
    lane = base + VEC * ((j - i) % VEC) + i
    return gram[:, lane : lane + 1]


def assemble(entries):
    lane, row = iota((VEC, LANES), 1), iota((VEC, LANES), 0)
    total = jnp.zeros((VEC, LANES), jnp.float32)
    for (i, j), value in entries.items():
        total = jnp.where((row == i) & (lane == j), value, total)
    return total


def factorize(gram, base):
    a = {(i, j): entry(gram, base, i, j) * (1.0 / ORDER) for i in range(VEC) for j in range(i + 1)}
    low, inv = {}, {}
    for j in range(VEC):
        pivot = a[j, j] + epsilon
        for k in range(j):
            pivot = pivot - low[j, k] * low[j, k]
        low[j, j] = jnp.sqrt(pivot)
        inv[j, j] = 1.0 / low[j, j]
        for i in range(j + 1, VEC):
            rest = a[i, j]
            for k in range(j):
                rest = rest - low[i, k] * low[j, k]
            low[i, j] = rest * inv[j, j]
    for j in range(VEC):
        for i in range(j + 1, VEC):
            rest = low[i, j] * inv[j, j]
            for k in range(j + 1, i):
                rest = rest + low[i, k] * inv[k, j]
            inv[i, j] = -rest * inv[i, i]
    flip = lambda entries: {(j, i): value for (i, j), value in entries.items()}
    return assemble(low), assemble(inv), assemble(flip(inv)), assemble(flip(low))


def projected(gram, inverse, inverse_t):
    entries = {}
    for i in range(VEC):
        for j in range(i + 1):
            value = (entry(gram, 0, i, j) + entry(gram, 0, j, i)) * (1.0 / ORDER)
            entries[i, j] = value
            entries[j, i] = value
    return apply(apply(inverse, assemble(entries)), inverse_t)


def split(block, row):
    high = block.astype(jnp.bfloat16).astype(jnp.float32)
    return jnp.where(row < VEC, high, block - high)


def twice(block):
    return jnp.concatenate([block, block], axis=0)


def kernel(
    x_hbm, tiles_hbm, rows_hbm, cols_hbm, count_hbm,
    basis_ref, resid_ref, coef_ref,
    x_ref, rows_ref, cols_ref, count_ref, raw, t_high, t_low, own, xr, xc, row_parts, col_parts, col_packed,
    fp, bp, fr, br, fm, bm, gsrc, gy, gp, isem, tsem, ssem, rsem,
):
    r, c = lax.axis_index("row"), lax.axis_index("col")
    y, core, z, x = lax.div(r, 2), lax.rem(r, 2), lax.div(c, 4), lax.rem(c, 4)
    group = 2 * r + lax.div(c, HALF)
    owner_row, owner_col = lax.div(c, 2), HALF * lax.rem(c, 2)
    lane_at = lax.rem(c, HALF)
    eight = iota((8, LANES), 0)

    turn = lax.rem(x + 4 - 2 * core, 4)
    odd = jnp.where((turn == 1) | (turn == 2), 1, 0)
    near = lax.rem(z + 9 - y, 8)
    keeper = near < 4
    kept_pair = jnp.where(keeper, near, 0) + jnp.where(turn >= 2, 4, 0)
    kept_group = 2 * r + odd

    def keeper_col(g, q):
        at_z = lax.rem(lax.div(g, 4) + 7 + lax.rem(q, 4), 8)
        at_x = lax.rem(g + 4 + (2 * lax.rem(g, 2) - 1) * lax.div(q, 4), 4)
        return 4 * at_z + at_x

    def send(src, dst, exchange, row, col):
        pltpu.make_async_remote_copy(
            src_ref=src, dst_ref=dst, send_sem=ssem.at[exchange], recv_sem=rsem.at[exchange],
            device_id=(row, col), device_id_type=MESH,
        ).start()

    def send_or_keep(src, dst, exchange, row, col):
        mine = (row == r) & (col == c)

        @pl.when(mine)
        def _():
            pltpu.make_async_copy(src, dst, rsem.at[exchange]).start()

        @pl.when(jnp.logical_not(mine))
        def _():
            send(src, dst, exchange, row, col)

    def wait(sem, ref):
        pltpu.make_async_copy(ref, ref, sem).wait()

    def loop(first, last, body):
        def step(j, carry):
            body(j)
            return carry
        lax.fori_loop(first, last, step, 0)

    def outward(j, size):
        return size // 2 + lax.div(j + 1, 2) * (1 - 2 * lax.rem(j, 2))

    def over_plane(body):
        def one(j):
            body(4 * lax.rem(z + outward(lax.div(j, 4), 8), 8) + lax.rem(x + outward(lax.rem(j, 4), 4), 4))
        loop(0, COLS - 1, one)

    def over_line(body, count=ROWS - 1):
        def one(j):
            body(2 * lax.rem(y + outward(lax.div(j, 2), 8), 8) + lax.rem(core + 1 + lax.rem(j, 2), 2))
        loop(0, count, one)

    pending = []

    pltpu.make_async_copy(x_hbm, x_ref, isem.at[0]).start()
    barrier = pltpu.get_barrier_semaphore()

    def greet(row, col):
        pl.semaphore_signal(barrier, 1, device_id=(row, col), device_id_type=MESH)

    over_line(lambda row: greet(row, group))

    @pl.when(owner_row != r)
    def _():
        loop(0, HALF, lambda j: greet(owner_row, owner_col + j))

    over_plane(lambda col: greet(r, col))
    for k in range(SLOTS):
        pltpu.make_async_copy(tiles_hbm.at[k], raw.at[k], tsem.at[k]).start()
    pltpu.make_async_copy(rows_hbm, rows_ref, isem.at[1]).start()
    pltpu.make_async_copy(cols_hbm, cols_ref, isem.at[2]).start()
    pltpu.make_async_copy(count_hbm, count_ref, isem.at[3]).start()
    wait(isem.at[0], x_ref)
    pl.semaphore_wait(barrier, jnp.where(owner_row != r, COLS - 1 + ROWS - 1 + HALF, COLS - 1 + ROWS - 1))

    def line_start(at, value, exchange):
        gsrc[2 * at] = value
        gy[at, r] = value
        over_line(lambda row: send(gsrc.at[2 * at], gy.at[at, r], exchange, row, c))
        pending.append((exchange, gy.at[at, pl.ds(0, ROWS - 1)], None))

    def plane_start(at, line_exchange, exchange):
        wait(rsem.at[line_exchange], gy.at[at, pl.ds(0, ROWS - 1)])
        value = jnp.sum(gy[at], axis=0)
        gsrc[2 * at + 1] = value
        gp[at, c] = value
        over_plane(lambda col: send(gsrc.at[2 * at + 1], gp.at[at, c], exchange, r, col))
        pending.append((exchange, gp.at[at, pl.ds(0, COLS - 1)], None))

    def plane_done(at, exchange):
        wait(rsem.at[exchange], gp.at[at, pl.ds(0, COLS - 1)])
        return jnp.sum(gp[at], axis=0)

    def spread(step, values, places, out, tiles):
        for t in range(tiles):
            total = jnp.where(places[0] == t, values[0], 0.0)
            for k in range(1, SLOTS):
                total = total + jnp.where(places[k] == t, values[k], 0.0)
            out[step, 2 * t] = total[:VEC]
            out[step, 2 * t + 1] = total[VEC:]

    def places():
        row_at = [lax.rem(rows_ref[k], ROW_TILES) for k in range(SLOTS)]
        col_at = [lax.rem(cols_ref[k], COL_TILES) for k in range(SLOTS)]
        masks = [jnp.where(k < count_ref[0], 1.0, 0.0).astype(jnp.float32) for k in range(SLOTS)]
        return row_at, col_at, masks

    def multiply(k, parts, at, dims, mask):
        block = parts[pl.ds(2 * at, 2)]
        block = jnp.concatenate([block[0], block[1]], axis=1).astype(jnp.bfloat16)
        high = lax.dot_general(block, t_high[k], (dims, ((), ())), preferred_element_type=jnp.float32)
        low = lax.dot_general(block, t_low[k], (dims, ((), ())), preferred_element_type=jnp.float32)
        both = high + low
        left, right = both[:, :LANES], both[:, LANES:]
        left = left + pltpu.roll(left, VEC, 0)
        right = right + pltpu.roll(right, VEC, 0)
        return jnp.where(eight < VEC, left, right) * mask

    def crossed(backward, col_at):
        cross = [jnp.zeros((8, LANES), jnp.float32) for _ in range(VEC)]
        for k in range(SLOTS):
            entries = col_packed[col_at[k]]
            for offset in range(VEC):
                cross[offset] = cross[offset] + entries * rotated(backward[k], offset)
        return gram_row(cross)

    def own_gram(block):
        block = twice(block)
        half = jnp.where(eight < VEC, block, 0.0)
        return gram_row([half * rotated(block, offset) for offset in range(VEC)])

    dst = xc.at[0, lane_at]
    over_line(lambda row: send(x_ref, dst, COL0, row, group))
    send_or_keep(x_ref, dst, COL0, r, group)
    over_plane(lambda col: send(x_ref, xr.at[0, c], ROW0, r, col))
    start = x_ref[...]
    xr[0, c] = start
    pending.append((ROW0, xr.at[0, pl.ds(0, COLS - 1)], None))
    pending.append((COL0, xc.at[0, pl.ds(0, ROWS - 1)], None))
    pending.append((COL0, xc.at[0, 0], group != c))

    def halve(k):
        wait(tsem.at[k], raw.at[k])
        tile = raw[k]
        high = tile.astype(jnp.bfloat16)
        t_high[k] = high
        t_low[k] = (tile - high.astype(jnp.float32)).astype(jnp.bfloat16)

    loop(0, SLOTS, halve)
    wait(isem.at[1], rows_ref)
    wait(isem.at[2], cols_ref)
    wait(isem.at[3], count_ref)
    row_at, col_at, masks = places()
    start_row = pltpu.roll(own_gram(start), 16, 1)
    wait(rsem.at[ROW0], xr.at[0, pl.ds(0, COLS - 1)])
    for t in range(COLS):
        row_parts[t] = split(twice(xr[0, t]), eight)
    backward = [multiply(k, row_parts, row_at[k], ((1,), (0,)), masks[k]) for k in range(SLOTS)]
    spread(0, backward, col_at, bp, COL_TILES)

    def to_keeper(j):
        send_or_keep(bp.at[0, pl.ds(14 - 2 * j, 2)], bm.at[r], BWD0, owner_row, keeper_col(c, 7 - j))

    loop(0, 8, to_keeper)
    wait(rsem.at[COL0], xc.at[0])
    for t in range(COL_TILES):
        left, right = twice(xc[0, 2 * t]), twice(xc[0, 2 * t + 1])
        col_parts[2 * t] = split(left, eight)
        col_parts[2 * t + 1] = split(right, eight)
        col_packed[t] = jnp.where(eight < VEC, left, right)
    line_start(0, crossed(backward, col_at) + start_row, LINE0)
    forward = [multiply(k, col_parts, col_at[k], ((1,), (1,)), masks[k]) for k in range(SLOTS)]
    spread(0, forward, row_at, fp, ROW_TILES)
    loop(0, HALF, lambda q: send_or_keep(
        fp.at[0, pl.ds(2 * q, 2)], fm.at[c], FWD0, r, keeper_col(2 * r + lax.div(q, 8), lax.rem(q, 8))))
    pending.append((BWD0, bp.at[0, pl.ds(0, HALF - 2)], None))
    pending.append((BWD0, bp.at[0, pl.ds(0, 2)], jnp.logical_not(keeper & (kept_group == c))))
    pending.append((FWD0, fp.at[0, pl.ds(0, COLS - 2)], None))
    pending.append((FWD0, fp.at[0, pl.ds(0, 2)], jnp.logical_not(keeper)))
    plane_start(0, LINE0, PLANE0)

    kept_at = HALF * odd + 2 * kept_pair
    at_row = xr.at[1, pl.ds(kept_at, 2)]
    at_col = xc.at[1, pl.ds(2 * kept_pair, 2)]

    @pl.when(keeper)
    def _():
        wait(rsem.at[FWD0], fm)
        total = jnp.sum(fm[...], axis=0)
        wait(rsem.at[BWD0], bm)
        own[...] = total + jnp.sum(bm[...], axis=0)
        over_line(lambda row: send_or_keep(own, at_col, COL1, row, kept_group), ROWS)
        over_plane(lambda col: send(own, at_row, ROW1, r, col))
        pltpu.make_async_copy(own, at_row, rsem.at[ROW1]).start()

    for lap in range(2):
        pending.append((ROW1, xr.at[1, pl.ds(0, COLS - 1)], keeper))
    pending.append((COL1, xc.at[1, pl.ds(0, HALF)], keeper))
    pending.append((COL1, xc.at[1, pl.ds(0, HALF - 2)], keeper))
    pending.append((COL1, xc.at[1, pl.ds(0, 2)], keeper & (kept_group != c)))

    gram = plane_done(0, PLANE0)
    _, inverse, inverse_t, _ = factorize(gram, 16)
    first_diag = projected(gram, inverse, inverse_t)
    first_basis = apply(inverse, start)
    from_start = -apply(first_diag, inverse)
    inverse_twice, start_factor_twice = twice(inverse), twice(from_start)
    of_image = [jnp.broadcast_to(inverse_twice[:, j : j + 1], (8, LANES)) for j in range(VEC)]
    of_start = [jnp.broadcast_to(start_factor_twice[:, j : j + 1], (8, LANES)) for j in range(VEC)]

    def combined(ref, at):
        total = of_image[0] * ref[1, at, 0:1, :] + of_start[0] * ref[0, at, 0:1, :]
        for j in range(1, VEC):
            total = total + (of_image[j] * ref[1, at, j : j + 1, :] + of_start[j] * ref[0, at, j : j + 1, :])
        return total

    kept = [apply(inverse, own[at]) + apply(from_start, xr[0, kept_at + at]) for at in range(2)]
    rest_row = own_gram(kept[0]) + own_gram(kept[1])
    line_start(1, jnp.where(keeper, rest_row, 0.0), LINE1)
    wait(rsem.at[ROW1], xr.at[1])
    for t in range(COLS):
        row_parts[t] = split(combined(xr, t), eight)
    backward = [multiply(k, row_parts, row_at[k], ((1,), (0,)), masks[k]) for k in range(SLOTS)]
    spread(1, backward, col_at, bp, COL_TILES)

    def back(j):
        s = lax.rem(c + j, HALF)
        send_or_keep(bp.at[1, s], br.at[r], BWD1, owner_row, owner_col + s)

    loop(0, HALF, back)
    wait(rsem.at[COL1], xc.at[1])
    for t in range(COL_TILES):
        left, right = combined(xc, 2 * t), combined(xc, 2 * t + 1)
        col_parts[2 * t] = split(left, eight)
        col_parts[2 * t + 1] = split(right, eight)
        col_packed[t] = jnp.where(eight < VEC, left, right)
    line_start(2, crossed(backward, col_at), LINE2)
    forward = [multiply(k, col_parts, col_at[k], ((1,), (1,)), masks[k]) for k in range(SLOTS)]
    spread(1, forward, row_at, fp, ROW_TILES)
    over_plane(lambda col: send(fp.at[1, col], fr.at[c], FWD1, r, col))
    fr[c] = fp[1, c]
    pending.append((FWD1, fr.at[pl.ds(0, COLS - 1)], None))
    pending.append((BWD1, br.at[pl.ds(0, HALF - 1)], None))
    pending.append((BWD1, br.at[0], group != c))
    plane_start(1, LINE1, PLANE1)
    plane_start(2, LINE2, PLANE2)
    gram = plane_done(1, PLANE1)
    rest = apply(inverse, xr[1, c]) + apply(from_start, start)
    factor, inverse, inverse_t, factor_t = factorize(gram, 0)
    next_basis = apply(inverse, rest)
    basis_ref[...] = next_basis
    wait(rsem.at[FWD1], fr.at[pl.ds(0, COLS - 1)])
    image = jnp.sum(fr[...], axis=0)
    wait(rsem.at[BWD1], br)
    image = image + jnp.sum(br[...], axis=0)
    known = apply(inverse, image) - apply(factor_t, first_basis)
    for exchange, ref, condition in pending[:-1]:
        if condition is None:
            wait(ssem.at[exchange], ref)
        else:
            pl.when(condition)(lambda exchange=exchange, ref=ref: wait(ssem.at[exchange], ref))
    gram = plane_done(2, PLANE2)
    second_diag = projected(gram, inverse, inverse_t)
    resid_ref[...] = known - apply(second_diag, next_basis)
    coef_ref[0] = first_diag[:, :VEC]
    coef_ref[1] = second_diag[:, :VEC]
    coef_ref[2] = factor[:, :VEC]
    wait(ssem.at[pending[-1][0]], pending[-1][1])


def settle(basis, resid, coef, basis_out, resid_out, coef_out, sem):
    copies = [
        pltpu.make_async_copy(src, dst, sem.at[at])
        for at, (src, dst) in enumerate(((basis, basis_out), (resid, resid_out), (coef, coef_out)))
    ]
    for copy in copies:
        copy.start()
    for copy in copies:
        copy.wait()


def body(start_block, matrix_tiles, tile_rows, tile_cols, tile_counts):
    share = jax.ShapeDtypeStruct((VEC, LANES), jnp.float32)
    shapes = (share, share, jax.ShapeDtypeStruct((3, VEC, VEC), jnp.float32))
    vmem, anywhere = pl.BlockSpec(memory_space=pltpu.VMEM), pl.BlockSpec(memory_space=pl.ANY)
    buffer = lambda *shape: pltpu.VMEM(shape, jnp.float32)
    found = pl.pallas_call(
        kernel,
        out_shape=tuple(pltpu.VMEM(shape.shape, shape.dtype) for shape in shapes),
        in_specs=[anywhere] * 5,
        out_specs=(vmem, vmem, vmem),
        scratch_shapes=[
            buffer(VEC, LANES),
            pltpu.SMEM((SLOTS,), jnp.int32),
            pltpu.SMEM((SLOTS,), jnp.int32),
            pltpu.SMEM((1,), jnp.int32),
            buffer(SLOTS, TILE, TILE),
            pltpu.VMEM((SLOTS, TILE, TILE), jnp.bfloat16),
            pltpu.VMEM((SLOTS, TILE, TILE), jnp.bfloat16),
            buffer(2, VEC, LANES),
            buffer(2, COLS, VEC, LANES),
            buffer(2, HALF, VEC, LANES),
            buffer(COLS, 8, LANES),
            buffer(HALF, 8, LANES),
            buffer(COL_TILES, 8, LANES),
            buffer(2, COLS, VEC, LANES),
            buffer(2, HALF, VEC, LANES),
            buffer(COLS, VEC, LANES),
            buffer(ROWS, VEC, LANES),
            buffer(COLS, 2, VEC, LANES),
            buffer(ROWS, 2, VEC, LANES),
            buffer(6, 1, LANES),
            buffer(3, ROWS, 1, LANES),
            buffer(3, COLS, 1, LANES),
            pltpu.SemaphoreType.DMA((4,)),
            pltpu.SemaphoreType.DMA((SLOTS,)),
            pltpu.SemaphoreType.DMA((14,)),
            pltpu.SemaphoreType.DMA((14,)),
        ],
        compiler_params=pltpu.CompilerParams(collective_id=0, has_side_effects=True),
    )(start_block, matrix_tiles, tile_rows, tile_cols, tile_counts)
    return pl.pallas_call(
        settle,
        out_shape=shapes,
        in_specs=[vmem] * 3,
        out_specs=(anywhere, anywhere, anywhere),
        scratch_shapes=[pltpu.SemaphoreType.DMA((3,))],
    )(*[pltpu.with_memory_space_constraint(f, pltpu.VMEM) for f in found])


def solution(mesh):
    return jax.shard_map(
        body,
        mesh=mesh,
        in_specs=(
            P(None, ("row", "col")),
            P(("row", "col"), None, None),
            P(("row", "col")),
            P(("row", "col")),
            P(("row", "col")),
        ),
        out_specs=(P(None, ("row", "col")), P(None, ("row", "col")), P()),
        check_vma=False,
    )
```

```python
import jax
import jax.numpy as jnp
from jax import lax
from jax.experimental import pallas as pl
from jax.experimental.pallas import tpu as pltpu
from jax.sharding import PartitionSpec as P

MESH = pl.DeviceIdType.MESH
epsilon = 1e-06
VEC, TILE, SLOTS, LANES = 4, 256, 8, 128
ROWS, COLS = 16, 32
HALF = COLS // 2
ROW_TILES, COL_TILES = 16, 8
ORDER = ROWS * COLS * LANES
SPAN, BELOW, WIDE = 8, 3, 1
KEPT = HALF // (SPAN * WIDE)
PARTS = SPAN * WIDE

ROW0, COL0, FWD0, BWD0, ROW1, COL1, FWD1, BWD1, PLANE0, LINE0, PLANE1, LINE1, PLANE2, LINE2 = range(14)


def iota(shape, axis):
    return lax.broadcasted_iota(jnp.int32, shape, axis)


def apply(matrix, block):
    return sum(matrix[:, j : j + 1] * block[j : j + 1, :] for j in range(VEC))


def rotated(block, offset):
    if offset == 0:
        return block
    keep = iota((8, LANES), 0) % VEC + offset < VEC
    return jnp.where(keep, pltpu.roll(block, 8 - offset, 0), pltpu.roll(block, VEC - offset, 0))


def gram_row(products):
    total = jnp.zeros((8, LANES), jnp.float32)
    lane, row = iota((8, LANES), 1), iota((8, LANES), 0)
    for offset, product in enumerate(products):
        summed = jnp.sum(product, axis=1, keepdims=True)
        total = jnp.where(lane == VEC * offset + row % VEC, summed, total)
    return jnp.sum(total, axis=0, keepdims=True)


def entry(gram, base, i, j):
    lane = base + VEC * ((j - i) % VEC) + i
    return gram[:, lane : lane + 1]


def assemble(entries):
    lane, row = iota((VEC, LANES), 1), iota((VEC, LANES), 0)
    total = jnp.zeros((VEC, LANES), jnp.float32)
    for (i, j), value in entries.items():
        total = jnp.where((row == i) & (lane == j), value, total)
    return total


def factorize(gram, base):
    a = {(i, j): entry(gram, base, i, j) * (1.0 / ORDER) for i in range(VEC) for j in range(i + 1)}
    low, inv = {}, {}
    for j in range(VEC):
        pivot = a[j, j] + epsilon
        for k in range(j):
            pivot = pivot - low[j, k] * low[j, k]
        low[j, j] = jnp.sqrt(pivot)
        inv[j, j] = 1.0 / low[j, j]
        for i in range(j + 1, VEC):
            rest = a[i, j]
            for k in range(j):
                rest = rest - low[i, k] * low[j, k]
            low[i, j] = rest * inv[j, j]
    for j in range(VEC):
        for i in range(j + 1, VEC):
            rest = low[i, j] * inv[j, j]
            for k in range(j + 1, i):
                rest = rest + low[i, k] * inv[k, j]
            inv[i, j] = -rest * inv[i, i]
    flip = lambda entries: {(j, i): value for (i, j), value in entries.items()}
    return assemble(low), assemble(inv), assemble(flip(inv)), assemble(flip(low))


def projected(gram, inverse, inverse_t):
    entries = {}
    for i in range(VEC):
        for j in range(i + 1):
            value = (entry(gram, 0, i, j) + entry(gram, 0, j, i)) * (1.0 / ORDER)
            entries[i, j] = value
            entries[j, i] = value
    return apply(apply(inverse, assemble(entries)), inverse_t)


def split(block, row):
    high = block.astype(jnp.bfloat16).astype(jnp.float32)
    return jnp.where(row < VEC, high, block - high)


def twice(block):
    return jnp.concatenate([block, block], axis=0)


def kernel(
    x_hbm, tiles_hbm, rows_hbm, cols_hbm, count_hbm,
    basis_ref, resid_ref, coef_ref,
    x_ref, rows_ref, cols_ref, count_ref, raw, t_high, t_low, own, xr, xc, row_parts, col_parts, col_packed,
    fp, bp, fr, br, fm, bm, gsrc, gy, gp, isem, tsem, ssem, rsem,
):
    r, c = lax.axis_index("row"), lax.axis_index("col")
    y, core, z, x = lax.div(r, 2), lax.rem(r, 2), lax.div(c, 4), lax.rem(c, 4)
    group = 2 * r + lax.div(c, HALF)
    owner_row, owner_col = lax.div(c, 2), HALF * lax.rem(c, 2)
    lane_at = lax.rem(c, HALF)
    eight = iota((8, LANES), 0)

    turn = lax.rem(x + 4 - 2 * core, 4)
    odd = jnp.where((turn == 1) | (turn == 2), 1, 0)
    near = lax.rem(z + 8 + BELOW - y, 8)
    keeper = (near < SPAN) & (turn < 2 * WIDE)
    kept_part = jnp.where(keeper, near + jnp.where(turn >= 2, SPAN, 0), 0)
    kept_group = 2 * r + odd

    def keeper_col(g, q):
        at_z = lax.rem(lax.div(g, 4) + 8 - BELOW + lax.rem(q, SPAN), 8)
        at_x = lax.rem(g + 4 + (2 * lax.rem(g, 2) - 1) * lax.div(q, SPAN), 4)
        return 4 * at_z + at_x

    def send(src, dst, exchange, row, col):
        pltpu.make_async_remote_copy(
            src_ref=src, dst_ref=dst, send_sem=ssem.at[exchange], recv_sem=rsem.at[exchange],
            device_id=(row, col), device_id_type=MESH,
        ).start()

    def send_or_keep(src, dst, exchange, row, col):
        mine = (row == r) & (col == c)

        @pl.when(mine)
        def _():
            pltpu.make_async_copy(src, dst, rsem.at[exchange]).start()

        @pl.when(jnp.logical_not(mine))
        def _():
            send(src, dst, exchange, row, col)

    def wait(sem, ref):
        pltpu.make_async_copy(ref, ref, sem).wait()

    def loop(first, last, body):
        def step(j, carry):
            body(j)
            return carry
        lax.fori_loop(first, last, step, 0)

    def outward(j, size):
        return size // 2 + lax.div(j + 1, 2) * (1 - 2 * lax.rem(j, 2))

    def over_plane(body, first=0, last=COLS - 1):
        def one(j):
            body(4 * lax.rem(z + outward(lax.div(j, 4), 8), 8) + lax.rem(x + outward(lax.rem(j, 4), 4), 4))
        loop(first, last, one)

    def over_line(body, count=ROWS - 1):
        def one(j):
            body(2 * lax.rem(y + outward(lax.div(j, 2), 8), 8) + lax.rem(core + 1 + lax.rem(j, 2), 2))
        loop(0, count, one)

    pending = []

    pltpu.make_async_copy(x_hbm, x_ref, isem.at[0]).start()
    barrier = pltpu.get_barrier_semaphore()

    def greet(row, col):
        pl.semaphore_signal(barrier, 1, device_id=(row, col), device_id_type=MESH)

    over_line(lambda row: greet(row, group))

    @pl.when(owner_row != r)
    def _():
        loop(0, HALF, lambda j: greet(owner_row, owner_col + j))

    over_plane(lambda col: greet(r, col))
    for k in range(SLOTS):
        pltpu.make_async_copy(tiles_hbm.at[k], raw.at[k], tsem.at[k]).start()
    pltpu.make_async_copy(rows_hbm, rows_ref, isem.at[1]).start()
    pltpu.make_async_copy(cols_hbm, cols_ref, isem.at[2]).start()
    pltpu.make_async_copy(count_hbm, count_ref, isem.at[3]).start()
    wait(isem.at[0], x_ref)
    pl.semaphore_wait(barrier, jnp.where(owner_row != r, COLS - 1 + ROWS - 1 + HALF, COLS - 1 + ROWS - 1))

    def line_start(at, value, exchange):
        gsrc[2 * at] = value
        gy[at, r] = value
        over_line(lambda row: send(gsrc.at[2 * at], gy.at[at, r], exchange, row, c))
        pending.append((exchange, gy.at[at, pl.ds(0, ROWS - 1)], None))

    def plane_start(at, line_exchange, exchange):
        wait(rsem.at[line_exchange], gy.at[at, pl.ds(0, ROWS - 1)])
        value = jnp.sum(gy[at], axis=0)
        gsrc[2 * at + 1] = value
        gp[at, c] = value
        over_plane(lambda col: send(gsrc.at[2 * at + 1], gp.at[at, c], exchange, r, col))
        pending.append((exchange, gp.at[at, pl.ds(0, COLS - 1)], None))

    def plane_done(at, exchange):
        wait(rsem.at[exchange], gp.at[at, pl.ds(0, COLS - 1)])
        return jnp.sum(gp[at], axis=0)

    def spread(step, values, places, out, tiles):
        for t in range(tiles):
            total = jnp.where(places[0] == t, values[0], 0.0)
            for k in range(1, SLOTS):
                total = total + jnp.where(places[k] == t, values[k], 0.0)
            out[step, 2 * t] = total[:VEC]
            out[step, 2 * t + 1] = total[VEC:]

    def places():
        row_at = [lax.rem(rows_ref[k], ROW_TILES) for k in range(SLOTS)]
        col_at = [lax.rem(cols_ref[k], COL_TILES) for k in range(SLOTS)]
        masks = [jnp.where(k < count_ref[0], 1.0, 0.0).astype(jnp.float32) for k in range(SLOTS)]
        return row_at, col_at, masks

    def multiply(k, parts, at, dims, mask):
        block = parts[pl.ds(2 * at, 2)]
        block = jnp.concatenate([block[0], block[1]], axis=1).astype(jnp.bfloat16)
        high = lax.dot_general(block, t_high[k], (dims, ((), ())), preferred_element_type=jnp.float32)
        low = lax.dot_general(block, t_low[k], (dims, ((), ())), preferred_element_type=jnp.float32)
        both = high + low
        left, right = both[:, :LANES], both[:, LANES:]
        left = left + pltpu.roll(left, VEC, 0)
        right = right + pltpu.roll(right, VEC, 0)
        return jnp.where(eight < VEC, left, right) * mask

    def crossed(backward, col_at):
        cross = [jnp.zeros((8, LANES), jnp.float32) for _ in range(VEC)]
        for k in range(SLOTS):
            entries = col_packed[col_at[k]]
            for offset in range(VEC):
                cross[offset] = cross[offset] + entries * rotated(backward[k], offset)
        return gram_row(cross)

    def own_gram(block):
        block = twice(block)
        half = jnp.where(eight < VEC, block, 0.0)
        return gram_row([half * rotated(block, offset) for offset in range(VEC)])

    dst = xc.at[0, lane_at]
    over_line(lambda row: send(x_ref, dst, COL0, row, group))
    send_or_keep(x_ref, dst, COL0, r, group)
    over_plane(lambda col: send(x_ref, xr.at[0, c], ROW0, r, col))
    start = x_ref[...]
    xr[0, c] = start
    pending.append((ROW0, xr.at[0, pl.ds(0, COLS - 1)], None))
    pending.append((COL0, xc.at[0, pl.ds(0, ROWS - 1)], None))
    pending.append((COL0, xc.at[0, 0], group != c))

    def halve(k):
        wait(tsem.at[k], raw.at[k])
        tile = raw[k]
        high = tile.astype(jnp.bfloat16)
        t_high[k] = high
        t_low[k] = (tile - high.astype(jnp.float32)).astype(jnp.bfloat16)

    loop(0, SLOTS, halve)
    wait(isem.at[1], rows_ref)
    wait(isem.at[2], cols_ref)
    wait(isem.at[3], count_ref)
    row_at, col_at, masks = places()
    start_row = pltpu.roll(own_gram(start), 16, 1)
    wait(rsem.at[ROW0], xr.at[0, pl.ds(0, COLS - 1)])
    for t in range(COLS):
        row_parts[t] = split(twice(xr[0, t]), eight)
    backward = [multiply(k, row_parts, row_at[k], ((1,), (0,)), masks[k]) for k in range(SLOTS)]
    spread(0, backward, col_at, bp, COL_TILES)

    def to_keeper(j):
        q = PARTS - 1 - j
        send_or_keep(bp.at[0, pl.ds(KEPT * q, KEPT)], bm.at[r], BWD0, owner_row, keeper_col(c, q))

    loop(0, PARTS, to_keeper)
    wait(rsem.at[COL0], xc.at[0])
    for t in range(COL_TILES):
        left, right = twice(xc[0, 2 * t]), twice(xc[0, 2 * t + 1])
        col_parts[2 * t] = split(left, eight)
        col_parts[2 * t + 1] = split(right, eight)
        col_packed[t] = jnp.where(eight < VEC, left, right)
    forward = [multiply(k, col_parts, col_at[k], ((1,), (1,)), masks[k]) for k in range(SLOTS)]
    spread(0, forward, row_at, fp, ROW_TILES)
    loop(0, 2 * PARTS, lambda q: send_or_keep(
        fp.at[0, pl.ds(KEPT * q, KEPT)], fm.at[c], FWD0, r, keeper_col(2 * r + lax.div(q, PARTS), lax.rem(q, PARTS))))
    line_start(0, crossed(backward, col_at) + start_row, LINE0)
    pending.append((BWD0, bp.at[0, pl.ds(0, HALF - KEPT)], None))
    pending.append((BWD0, bp.at[0, pl.ds(0, KEPT)], jnp.logical_not(keeper & (kept_group == c))))
    pending.append((FWD0, fp.at[0, pl.ds(0, COLS - KEPT)], None))
    pending.append((FWD0, fp.at[0, pl.ds(0, KEPT)], jnp.logical_not(keeper)))
    plane_start(0, LINE0, PLANE0)

    kept_at = HALF * odd + KEPT * kept_part
    at_row = xr.at[1, pl.ds(kept_at, KEPT)]
    at_col = xc.at[1, pl.ds(KEPT * kept_part, KEPT)]

    @pl.when(keeper)
    def _():
        wait(rsem.at[FWD0], fm)
        total = jnp.sum(fm[...], axis=0)
        wait(rsem.at[BWD0], bm)
        own[...] = total + jnp.sum(bm[...], axis=0)
        over_plane(lambda col: send(own, at_row, ROW1, r, col))
        over_line(lambda row: send_or_keep(own, at_col, COL1, row, kept_group), ROWS)
        pltpu.make_async_copy(own, at_row, rsem.at[ROW1]).start()

    for lap in range(KEPT):
        pending.append((ROW1, xr.at[1, pl.ds(0, COLS - 1)], keeper))
        pending.append((COL1, xc.at[1, pl.ds(0, ROWS - 1)], keeper))
    pending.append((COL1, xc.at[1, pl.ds(0, KEPT)], keeper & (kept_group != c)))

    gram = plane_done(0, PLANE0)
    _, inverse, inverse_t, _ = factorize(gram, 16)
    first_diag = projected(gram, inverse, inverse_t)
    first_basis = apply(inverse, start)
    from_start = -apply(first_diag, inverse)
    inverse_twice, start_factor_twice = twice(inverse), twice(from_start)
    of_image = [jnp.broadcast_to(inverse_twice[:, j : j + 1], (8, LANES)) for j in range(VEC)]
    of_start = [jnp.broadcast_to(start_factor_twice[:, j : j + 1], (8, LANES)) for j in range(VEC)]

    def combined(ref, at):
        total = of_image[0] * ref[1, at, 0:1, :] + of_start[0] * ref[0, at, 0:1, :]
        for j in range(1, VEC):
            total = total + (of_image[j] * ref[1, at, j : j + 1, :] + of_start[j] * ref[0, at, j : j + 1, :])
        return total

    kept = [apply(inverse, own[at]) + apply(from_start, xr[0, kept_at + at]) for at in range(KEPT)]
    rest_row = sum(own_gram(block) for block in kept)
    line_start(1, jnp.where(keeper, rest_row, 0.0), LINE1)
    wait(rsem.at[ROW1], xr.at[1])
    for t in range(COLS):
        row_parts[t] = split(combined(xr, t), eight)
    backward = [multiply(k, row_parts, row_at[k], ((1,), (0,)), masks[k]) for k in range(SLOTS)]
    spread(1, backward, col_at, bp, COL_TILES)

    def back(j):
        s = lax.rem(c + j, HALF)
        send_or_keep(bp.at[1, s], br.at[r], BWD1, owner_row, owner_col + s)

    loop(0, HALF, back)
    wait(rsem.at[COL1], xc.at[1])
    for t in range(COL_TILES):
        left, right = combined(xc, 2 * t), combined(xc, 2 * t + 1)
        col_parts[2 * t] = split(left, eight)
        col_parts[2 * t + 1] = split(right, eight)
        col_packed[t] = jnp.where(eight < VEC, left, right)
    line_start(2, crossed(backward, col_at), LINE2)
    forward = [multiply(k, col_parts, col_at[k], ((1,), (1,)), masks[k]) for k in range(SLOTS)]
    spread(1, forward, row_at, fp, ROW_TILES)
    over_plane(lambda col: send(fp.at[1, col], fr.at[c], FWD1, r, col))
    fr[c] = fp[1, c]
    pending.append((FWD1, fr.at[pl.ds(0, COLS - 1)], None))
    pending.append((BWD1, br.at[pl.ds(0, HALF - 1)], None))
    pending.append((BWD1, br.at[0], group != c))
    plane_start(1, LINE1, PLANE1)
    plane_start(2, LINE2, PLANE2)
    gram = plane_done(1, PLANE1)
    rest = apply(inverse, xr[1, c]) + apply(from_start, start)
    factor, inverse, inverse_t, factor_t = factorize(gram, 0)
    next_basis = apply(inverse, rest)
    basis_ref[...] = next_basis
    wait(rsem.at[FWD1], fr.at[pl.ds(0, COLS - 1)])
    image = jnp.sum(fr[...], axis=0)
    wait(rsem.at[BWD1], br)
    image = image + jnp.sum(br[...], axis=0)
    known = apply(inverse, image) - apply(factor_t, first_basis)
    for exchange, ref, condition in pending[:-1]:
        if condition is None:
            wait(ssem.at[exchange], ref)
        else:
            pl.when(condition)(lambda exchange=exchange, ref=ref: wait(ssem.at[exchange], ref))
    gram = plane_done(2, PLANE2)
    second_diag = projected(gram, inverse, inverse_t)
    resid_ref[...] = known - apply(second_diag, next_basis)
    coef_ref[0] = first_diag[:, :VEC]
    coef_ref[1] = second_diag[:, :VEC]
    coef_ref[2] = factor[:, :VEC]
    wait(ssem.at[pending[-1][0]], pending[-1][1])


def settle(basis, resid, coef, basis_out, resid_out, coef_out, sem):
    copies = [
        pltpu.make_async_copy(src, dst, sem.at[at])
        for at, (src, dst) in enumerate(((basis, basis_out), (resid, resid_out), (coef, coef_out)))
    ]
    for copy in copies:
        copy.start()
    for copy in copies:
        copy.wait()


def body(start_block, matrix_tiles, tile_rows, tile_cols, tile_counts):
    share = jax.ShapeDtypeStruct((VEC, LANES), jnp.float32)
    shapes = (share, share, jax.ShapeDtypeStruct((3, VEC, VEC), jnp.float32))
    vmem, anywhere = pl.BlockSpec(memory_space=pltpu.VMEM), pl.BlockSpec(memory_space=pl.ANY)
    buffer = lambda *shape: pltpu.VMEM(shape, jnp.float32)
    found = pl.pallas_call(
        kernel,
        out_shape=tuple(pltpu.VMEM(shape.shape, shape.dtype) for shape in shapes),
        in_specs=[anywhere] * 5,
        out_specs=(vmem, vmem, vmem),
        scratch_shapes=[
            buffer(VEC, LANES),
            pltpu.SMEM((SLOTS,), jnp.int32),
            pltpu.SMEM((SLOTS,), jnp.int32),
            pltpu.SMEM((1,), jnp.int32),
            buffer(SLOTS, TILE, TILE),
            pltpu.VMEM((SLOTS, TILE, TILE), jnp.bfloat16),
            pltpu.VMEM((SLOTS, TILE, TILE), jnp.bfloat16),
            buffer(KEPT, VEC, LANES),
            buffer(2, COLS, VEC, LANES),
            buffer(2, HALF, VEC, LANES),
            buffer(COLS, 8, LANES),
            buffer(HALF, 8, LANES),
            buffer(COL_TILES, 8, LANES),
            buffer(2, COLS, VEC, LANES),
            buffer(2, HALF, VEC, LANES),
            buffer(COLS, VEC, LANES),
            buffer(ROWS, VEC, LANES),
            buffer(COLS, KEPT, VEC, LANES),
            buffer(ROWS, KEPT, VEC, LANES),
            buffer(6, 1, LANES),
            buffer(3, ROWS, 1, LANES),
            buffer(3, COLS, 1, LANES),
            pltpu.SemaphoreType.DMA((4,)),
            pltpu.SemaphoreType.DMA((SLOTS,)),
            pltpu.SemaphoreType.DMA((14,)),
            pltpu.SemaphoreType.DMA((14,)),
        ],
        compiler_params=pltpu.CompilerParams(collective_id=0, has_side_effects=True),
    )(start_block, matrix_tiles, tile_rows, tile_cols, tile_counts)
    return pl.pallas_call(
        settle,
        out_shape=shapes,
        in_specs=[vmem] * 3,
        out_specs=(anywhere, anywhere, anywhere),
        scratch_shapes=[pltpu.SemaphoreType.DMA((3,))],
    )(*[pltpu.with_memory_space_constraint(f, pltpu.VMEM) for f in found])


def solution(mesh):
    return jax.shard_map(
        body,
        mesh=mesh,
        in_specs=(
            P(None, ("row", "col")),
            P(("row", "col"), None, None),
            P(("row", "col")),
            P(("row", "col")),
            P(("row", "col")),
        ),
        out_specs=(P(None, ("row", "col")), P(None, ("row", "col")), P()),
        check_vma=False,
    )
```

```python
import jax
import jax.numpy as jnp
from jax import lax
from jax.experimental import pallas as pl
from jax.experimental.pallas import tpu as pltpu
from jax.sharding import PartitionSpec as P

MESH = pl.DeviceIdType.MESH
epsilon = 1e-06
VEC, TILE, SLOTS, LANES = 4, 256, 8, 128
ROWS, COLS = 16, 32
HALF = COLS // 2
ROW_TILES, COL_TILES = 16, 8
ORDER = ROWS * COLS * LANES
KEPT = 2

ROW0, COL0, FWD0, BWD0, ROW1, COL1, FWD1, BWD1, PLANE0, LINE0, PLANE1, LINE1, PLANE2, LINE2 = range(14)


def iota(shape, axis):
    return lax.broadcasted_iota(jnp.int32, shape, axis)


def apply(matrix, block):
    return sum(matrix[:, j : j + 1] * block[j : j + 1, :] for j in range(VEC))


def rotated(block, offset):
    if offset == 0:
        return block
    keep = iota((8, LANES), 0) % VEC + offset < VEC
    return jnp.where(keep, pltpu.roll(block, 8 - offset, 0), pltpu.roll(block, VEC - offset, 0))


def gram_row(products):
    total = jnp.zeros((8, LANES), jnp.float32)
    lane, row = iota((8, LANES), 1), iota((8, LANES), 0)
    for offset, product in enumerate(products):
        summed = jnp.sum(product, axis=1, keepdims=True)
        total = jnp.where(lane == VEC * offset + row % VEC, summed, total)
    return jnp.sum(total, axis=0, keepdims=True)


def entry(gram, base, i, j):
    lane = base + VEC * ((j - i) % VEC) + i
    return gram[:, lane : lane + 1]


def assemble(entries):
    lane, row = iota((VEC, LANES), 1), iota((VEC, LANES), 0)
    total = jnp.zeros((VEC, LANES), jnp.float32)
    for (i, j), value in entries.items():
        total = jnp.where((row == i) & (lane == j), value, total)
    return total


def factorize(gram, base):
    a = {(i, j): entry(gram, base, i, j) * (1.0 / ORDER) for i in range(VEC) for j in range(i + 1)}
    low, inv = {}, {}
    for j in range(VEC):
        pivot = a[j, j] + epsilon
        for k in range(j):
            pivot = pivot - low[j, k] * low[j, k]
        low[j, j] = jnp.sqrt(pivot)
        inv[j, j] = 1.0 / low[j, j]
        for i in range(j + 1, VEC):
            rest = a[i, j]
            for k in range(j):
                rest = rest - low[i, k] * low[j, k]
            low[i, j] = rest * inv[j, j]
    for j in range(VEC):
        for i in range(j + 1, VEC):
            rest = low[i, j] * inv[j, j]
            for k in range(j + 1, i):
                rest = rest + low[i, k] * inv[k, j]
            inv[i, j] = -rest * inv[i, i]
    flip = lambda entries: {(j, i): value for (i, j), value in entries.items()}
    return assemble(low), assemble(inv), assemble(flip(inv)), assemble(flip(low))


def projected(gram, inverse, inverse_t):
    entries = {}
    for i in range(VEC):
        for j in range(i + 1):
            value = (entry(gram, 0, i, j) + entry(gram, 0, j, i)) * (1.0 / ORDER)
            entries[i, j] = value
            entries[j, i] = value
    return apply(apply(inverse, assemble(entries)), inverse_t)


def split(block, row):
    high = block.astype(jnp.bfloat16).astype(jnp.float32)
    return jnp.where(row < VEC, high, block - high)


def twice(block):
    return jnp.concatenate([block, block], axis=0)


def kernel(
    x_hbm, tiles_hbm, rows_hbm, cols_hbm, count_hbm,
    basis_ref, resid_ref, coef_ref,
    x_ref, rows_ref, cols_ref, count_ref, raw, t_high, t_low, own, xr, xc, row_parts, col_parts, col_packed,
    fp, bp, fr, br, fm, bm, gsrc, gy, gp, isem, tsem, ssem, rsem,
):
    r, c = lax.axis_index("row"), lax.axis_index("col")
    y, core, z, x = lax.div(r, 2), lax.rem(r, 2), lax.div(c, 4), lax.rem(c, 4)
    group = 2 * r + lax.div(c, HALF)
    owner_row, owner_col = lax.div(c, 2), HALF * lax.rem(c, 2)
    lane_at = lax.rem(c, HALF)
    eight = iota((8, LANES), 0)

    turn = lax.rem(x + 4 - 2 * core, 4)
    keeper = turn < 2
    odd = lax.rem(turn, 2)
    kept_part = lax.rem(z + 8 - y, 8)
    kept_group = 2 * r + odd

    def send(src, dst, exchange, row, col):
        pltpu.make_async_remote_copy(
            src_ref=src, dst_ref=dst, send_sem=ssem.at[exchange], recv_sem=rsem.at[exchange],
            device_id=(row, col), device_id_type=MESH,
        ).start()

    def send_or_keep(src, dst, exchange, row, col):
        mine = (row == r) & (col == c)

        @pl.when(mine)
        def _():
            pltpu.make_async_copy(src, dst, rsem.at[exchange]).start()

        @pl.when(jnp.logical_not(mine))
        def _():
            send(src, dst, exchange, row, col)

    def wait(sem, ref):
        pltpu.make_async_copy(ref, ref, sem).wait()

    def loop(first, last, body):
        def step(j, carry):
            body(j)
            return carry
        lax.fori_loop(first, last, step, 0)

    def outward(size):
        return [size // 2 + (j + 1) // 2 * (1 - 2 * (j % 2)) for j in range(size)]

    plane_z = [4 * lax.rem(z + away, 8) for away in outward(8)]
    plane_x = [lax.rem(x + away, 4) for away in outward(4)]
    line_y = [2 * lax.rem(y + away, 8) for away in outward(8)]
    line_core = [1 - core, core]

    def over_plane(body):
        for at in range(COLS - 1):
            body(plane_z[at // 4] + plane_x[at % 4])

    def over_line(body, count=ROWS - 1):
        for at in range(count):
            body(line_y[at // 2] + line_core[at % 2])

    pending = []

    pltpu.make_async_copy(x_hbm, x_ref, isem.at[0]).start()
    barrier = pltpu.get_barrier_semaphore()

    def greet(row, col):
        pl.semaphore_signal(barrier, 1, device_id=(row, col), device_id_type=MESH)

    over_line(lambda row: greet(row, group))

    @pl.when(owner_row != r)
    def _():
        for j in range(HALF):
            greet(owner_row, owner_col + j)

    over_plane(lambda col: greet(r, col))
    for k in range(SLOTS):
        pltpu.make_async_copy(tiles_hbm.at[k], raw.at[k], tsem.at[k]).start()
    pltpu.make_async_copy(rows_hbm, rows_ref, isem.at[1]).start()
    pltpu.make_async_copy(cols_hbm, cols_ref, isem.at[2]).start()
    pltpu.make_async_copy(count_hbm, count_ref, isem.at[3]).start()
    wait(isem.at[0], x_ref)
    pl.semaphore_wait(barrier, jnp.where(owner_row != r, COLS - 1 + ROWS - 1 + HALF, COLS - 1 + ROWS - 1))

    def line_start(at, value, exchange):
        gsrc[2 * at] = value
        gy[at, r] = value
        over_line(lambda row: send(gsrc.at[2 * at], gy.at[at, r], exchange, row, c))
        pending.append((exchange, gy.at[at, pl.ds(0, ROWS - 1)], None))

    def plane_start(at, line_exchange, exchange):
        wait(rsem.at[line_exchange], gy.at[at, pl.ds(0, ROWS - 1)])
        value = jnp.sum(gy[at], axis=0)
        gsrc[2 * at + 1] = value
        gp[at, c] = value
        over_plane(lambda col: send(gsrc.at[2 * at + 1], gp.at[at, c], exchange, r, col))
        pending.append((exchange, gp.at[at, pl.ds(0, COLS - 1)], None))

    def plane_done(at, exchange):
        wait(rsem.at[exchange], gp.at[at, pl.ds(0, COLS - 1)])
        return jnp.sum(gp[at], axis=0)

    def spread(step, values, places, out, tiles):
        for t in range(tiles):
            total = jnp.where(places[0] == t, values[0], 0.0)
            for k in range(1, SLOTS):
                total = total + jnp.where(places[k] == t, values[k], 0.0)
            out[step, 2 * t] = total[:VEC]
            out[step, 2 * t + 1] = total[VEC:]

    def places():
        row_at = [lax.rem(rows_ref[k], ROW_TILES) for k in range(SLOTS)]
        col_at = [lax.rem(cols_ref[k], COL_TILES) for k in range(SLOTS)]
        masks = [jnp.where(k < count_ref[0], 1.0, 0.0).astype(jnp.float32) for k in range(SLOTS)]
        return row_at, col_at, masks

    def multiply(k, parts, at, dims, mask):
        block = parts[pl.ds(2 * at, 2)]
        block = jnp.concatenate([block[0], block[1]], axis=1).astype(jnp.bfloat16)
        high = lax.dot_general(block, t_high[k], (dims, ((), ())), preferred_element_type=jnp.float32)
        low = lax.dot_general(block, t_low[k], (dims, ((), ())), preferred_element_type=jnp.float32)
        both = high + low
        left, right = both[:, :LANES], both[:, LANES:]
        left = left + pltpu.roll(left, VEC, 0)
        right = right + pltpu.roll(right, VEC, 0)
        return jnp.where(eight < VEC, left, right) * mask

    def crossed(backward, col_at):
        cross = [jnp.zeros((8, LANES), jnp.float32) for _ in range(VEC)]
        for k in range(SLOTS):
            entries = col_packed[col_at[k]]
            for offset in range(VEC):
                cross[offset] = cross[offset] + entries * rotated(backward[k], offset)
        return gram_row(cross)

    def own_gram(block):
        block = twice(block)
        half = jnp.where(eight < VEC, block, 0.0)
        return gram_row([half * rotated(block, offset) for offset in range(VEC)])

    dst = xc.at[0, lane_at]
    over_line(lambda row: send(x_ref, dst, COL0, row, group))
    send_or_keep(x_ref, dst, COL0, r, group)
    over_plane(lambda col: send(x_ref, xr.at[0, c], ROW0, r, col))
    start = x_ref[...]
    xr[0, c] = start
    pending.append((ROW0, xr.at[0, pl.ds(0, COLS - 1)], None))
    pending.append((COL0, xc.at[0, pl.ds(0, ROWS - 1)], None))
    pending.append((COL0, xc.at[0, 0], group != c))

    def halve(k):
        wait(tsem.at[k], raw.at[k])
        tile = raw[k]
        high = tile.astype(jnp.bfloat16)
        t_high[k] = high
        t_low[k] = (tile - high.astype(jnp.float32)).astype(jnp.bfloat16)

    loop(0, SLOTS, halve)
    wait(isem.at[1], rows_ref)
    wait(isem.at[2], cols_ref)
    wait(isem.at[3], count_ref)
    row_at, col_at, masks = places()
    start_row = pltpu.roll(own_gram(start), 16, 1)
    wait(rsem.at[ROW0], xr.at[0, pl.ds(0, COLS - 1)])
    for t in range(COLS):
        row_parts[t] = split(twice(xr[0, t]), eight)
    backward = [multiply(k, row_parts, row_at[k], ((1,), (0,)), masks[k]) for k in range(SLOTS)]
    spread(0, backward, col_at, bp, COL_TILES)

    for at, q in enumerate(outward(8)):
        send_or_keep(bp.at[0, pl.ds(KEPT * q, KEPT)], bm.at[r], BWD0, owner_row, plane_z[at] + x)
    wait(rsem.at[COL0], xc.at[0])
    for t in range(COL_TILES):
        left, right = twice(xc[0, 2 * t]), twice(xc[0, 2 * t + 1])
        col_parts[2 * t] = split(left, eight)
        col_parts[2 * t + 1] = split(right, eight)
        col_packed[t] = jnp.where(eight < VEC, left, right)
    forward = [multiply(k, col_parts, col_at[k], ((1,), (1,)), masks[k]) for k in range(SLOTS)]
    spread(0, forward, row_at, fp, ROW_TILES)
    for at, away in enumerate(outward(8)):
        q = lax.rem(z + 8 - y + away, 8)
        for half in range(2):
            part = fp.at[0, pl.ds(HALF * half + KEPT * q, KEPT)]
            send_or_keep(part, fm.at[c], FWD0, r, plane_z[at] + 2 * core + half)
    line_start(0, crossed(backward, col_at) + start_row, LINE0)
    pending.append((BWD0, bp.at[0, pl.ds(0, HALF - KEPT)], None))
    pending.append((BWD0, bp.at[0, pl.ds(0, KEPT)], jnp.logical_not(keeper & (kept_group == c))))
    pending.append((FWD0, fp.at[0, pl.ds(0, COLS - KEPT)], None))
    pending.append((FWD0, fp.at[0, pl.ds(0, KEPT)], jnp.logical_not(keeper)))
    plane_start(0, LINE0, PLANE0)

    kept_at = HALF * odd + KEPT * kept_part
    at_row = xr.at[1, pl.ds(kept_at, KEPT)]
    at_col = xc.at[1, pl.ds(KEPT * kept_part, KEPT)]

    @pl.when(keeper)
    def _():
        wait(rsem.at[FWD0], fm)
        total = jnp.sum(fm[...], axis=0)
        wait(rsem.at[BWD0], bm)
        own[...] = total + jnp.sum(bm[...], axis=0)
        over_plane(lambda col: send(own, at_row, ROW1, r, col))
        over_line(lambda row: send_or_keep(own, at_col, COL1, row, kept_group), ROWS)
        pltpu.make_async_copy(own, at_row, rsem.at[ROW1]).start()

    for lap in range(KEPT):
        pending.append((ROW1, xr.at[1, pl.ds(0, COLS - 1)], keeper))
        pending.append((COL1, xc.at[1, pl.ds(0, ROWS - 1)], keeper))
    pending.append((COL1, xc.at[1, pl.ds(0, KEPT)], keeper & (kept_group != c)))

    gram = plane_done(0, PLANE0)
    _, inverse, inverse_t, _ = factorize(gram, 16)
    first_diag = projected(gram, inverse, inverse_t)
    first_basis = apply(inverse, start)
    from_start = -apply(first_diag, inverse)
    inverse_twice, start_factor_twice = twice(inverse), twice(from_start)
    of_image = [jnp.broadcast_to(inverse_twice[:, j : j + 1], (8, LANES)) for j in range(VEC)]
    of_start = [jnp.broadcast_to(start_factor_twice[:, j : j + 1], (8, LANES)) for j in range(VEC)]

    def combined(ref, at):
        total = of_image[0] * ref[1, at, 0:1, :] + of_start[0] * ref[0, at, 0:1, :]
        for j in range(1, VEC):
            total = total + (of_image[j] * ref[1, at, j : j + 1, :] + of_start[j] * ref[0, at, j : j + 1, :])
        return total

    kept = [apply(inverse, own[at]) + apply(from_start, xr[0, kept_at + at]) for at in range(KEPT)]
    rest_row = sum(own_gram(block) for block in kept)
    line_start(1, jnp.where(keeper, rest_row, 0.0), LINE1)
    wait(rsem.at[ROW1], xr.at[1])
    for t in range(COLS):
        row_parts[t] = split(combined(xr, t), eight)
    backward = [multiply(k, row_parts, row_at[k], ((1,), (0,)), masks[k]) for k in range(SLOTS)]
    spread(1, backward, col_at, bp, COL_TILES)

    def back(j):
        s = lax.rem(c + j, HALF)
        send_or_keep(bp.at[1, s], br.at[r], BWD1, owner_row, owner_col + s)

    for j in range(HALF):
        back(j)
    wait(rsem.at[COL1], xc.at[1])
    for t in range(COL_TILES):
        left, right = combined(xc, 2 * t), combined(xc, 2 * t + 1)
        col_parts[2 * t] = split(left, eight)
        col_parts[2 * t + 1] = split(right, eight)
        col_packed[t] = jnp.where(eight < VEC, left, right)
    line_start(2, crossed(backward, col_at), LINE2)
    forward = [multiply(k, col_parts, col_at[k], ((1,), (1,)), masks[k]) for k in range(SLOTS)]
    spread(1, forward, row_at, fp, ROW_TILES)
    over_plane(lambda col: send(fp.at[1, col], fr.at[c], FWD1, r, col))
    fr[c] = fp[1, c]
    pending.append((FWD1, fr.at[pl.ds(0, COLS - 1)], None))
    pending.append((BWD1, br.at[pl.ds(0, HALF - 1)], None))
    pending.append((BWD1, br.at[0], group != c))
    plane_start(1, LINE1, PLANE1)
    plane_start(2, LINE2, PLANE2)
    gram = plane_done(1, PLANE1)
    rest = apply(inverse, xr[1, c]) + apply(from_start, start)
    factor, inverse, inverse_t, factor_t = factorize(gram, 0)
    next_basis = apply(inverse, rest)
    basis_ref[...] = next_basis
    wait(rsem.at[FWD1], fr.at[pl.ds(0, COLS - 1)])
    image = jnp.sum(fr[...], axis=0)
    wait(rsem.at[BWD1], br)
    image = image + jnp.sum(br[...], axis=0)
    known = apply(inverse, image) - apply(factor_t, first_basis)
    for exchange, ref, condition in pending[:-1]:
        if condition is None:
            wait(ssem.at[exchange], ref)
        else:
            pl.when(condition)(lambda exchange=exchange, ref=ref: wait(ssem.at[exchange], ref))
    gram = plane_done(2, PLANE2)
    second_diag = projected(gram, inverse, inverse_t)
    resid_ref[...] = known - apply(second_diag, next_basis)
    coef_ref[0] = first_diag[:, :VEC]
    coef_ref[1] = second_diag[:, :VEC]
    coef_ref[2] = factor[:, :VEC]
    wait(ssem.at[pending[-1][0]], pending[-1][1])


def settle(basis, resid, coef, basis_out, resid_out, coef_out, sem):
    copies = [
        pltpu.make_async_copy(src, dst, sem.at[at])
        for at, (src, dst) in enumerate(((basis, basis_out), (resid, resid_out), (coef, coef_out)))
    ]
    for copy in copies:
        copy.start()
    for copy in copies:
        copy.wait()


def body(start_block, matrix_tiles, tile_rows, tile_cols, tile_counts):
    share = jax.ShapeDtypeStruct((VEC, LANES), jnp.float32)
    shapes = (share, share, jax.ShapeDtypeStruct((3, VEC, VEC), jnp.float32))
    vmem, anywhere = pl.BlockSpec(memory_space=pltpu.VMEM), pl.BlockSpec(memory_space=pl.ANY)
    buffer = lambda *shape: pltpu.VMEM(shape, jnp.float32)
    found = pl.pallas_call(
        kernel,
        out_shape=tuple(pltpu.VMEM(shape.shape, shape.dtype) for shape in shapes),
        in_specs=[anywhere] * 5,
        out_specs=(vmem, vmem, vmem),
        scratch_shapes=[
            buffer(VEC, LANES),
            pltpu.SMEM((SLOTS,), jnp.int32),
            pltpu.SMEM((SLOTS,), jnp.int32),
            pltpu.SMEM((1,), jnp.int32),
            buffer(SLOTS, TILE, TILE),
            pltpu.VMEM((SLOTS, TILE, TILE), jnp.bfloat16),
            pltpu.VMEM((SLOTS, TILE, TILE), jnp.bfloat16),
            buffer(KEPT, VEC, LANES),
            buffer(2, COLS, VEC, LANES),
            buffer(2, HALF, VEC, LANES),
            buffer(COLS, 8, LANES),
            buffer(HALF, 8, LANES),
            buffer(COL_TILES, 8, LANES),
            buffer(2, COLS, VEC, LANES),
            buffer(2, HALF, VEC, LANES),
            buffer(COLS, VEC, LANES),
            buffer(ROWS, VEC, LANES),
            buffer(COLS, KEPT, VEC, LANES),
            buffer(ROWS, KEPT, VEC, LANES),
            buffer(6, 1, LANES),
            buffer(3, ROWS, 1, LANES),
            buffer(3, COLS, 1, LANES),
            pltpu.SemaphoreType.DMA((4,)),
            pltpu.SemaphoreType.DMA((SLOTS,)),
            pltpu.SemaphoreType.DMA((14,)),
            pltpu.SemaphoreType.DMA((14,)),
        ],
        compiler_params=pltpu.CompilerParams(collective_id=0, has_side_effects=True),
    )(start_block, matrix_tiles, tile_rows, tile_cols, tile_counts)
    return pl.pallas_call(
        settle,
        out_shape=shapes,
        in_specs=[vmem] * 3,
        out_specs=(anywhere, anywhere, anywhere),
        scratch_shapes=[pltpu.SemaphoreType.DMA((3,))],
    )(*[pltpu.with_memory_space_constraint(f, pltpu.VMEM) for f in found])


def solution(mesh):
    return jax.shard_map(
        body,
        mesh=mesh,
        in_specs=(
            P(None, ("row", "col")),
            P(("row", "col"), None, None),
            P(("row", "col")),
            P(("row", "col")),
            P(("row", "col")),
        ),
        out_specs=(P(None, ("row", "col")), P(None, ("row", "col")), P()),
        check_vma=False,
    )
```

```python
import jax
import jax.numpy as jnp
from jax import lax
from jax.experimental import pallas as pl
from jax.experimental.pallas import tpu as pltpu
from jax.sharding import PartitionSpec as P

MESH = pl.DeviceIdType.MESH
epsilon = 1e-06
VEC, TILE, SLOTS, LANES = 4, 256, 8, 128
ROWS, COLS = 16, 32
HALF = COLS // 2
ROW_TILES, COL_TILES = 16, 8
ORDER = ROWS * COLS * LANES
KEPT = 2

ROW0, COL0, FWD0, BWD0, ROW1, COL1, FWD1, BWD1, PLANE0, LINE0, PLANE1, LINE1, PLANE2, LINE2 = range(14)


def iota(shape, axis):
    return lax.broadcasted_iota(jnp.int32, shape, axis)


def apply(matrix, block):
    return sum(matrix[:, j : j + 1] * block[j : j + 1, :] for j in range(VEC))


def rotated(block, offset):
    if offset == 0:
        return block
    keep = iota((8, LANES), 0) % VEC + offset < VEC
    return jnp.where(keep, pltpu.roll(block, 8 - offset, 0), pltpu.roll(block, VEC - offset, 0))


def gram_row(products):
    total = jnp.zeros((8, LANES), jnp.float32)
    lane, row = iota((8, LANES), 1), iota((8, LANES), 0)
    for offset, product in enumerate(products):
        summed = jnp.sum(product, axis=1, keepdims=True)
        total = jnp.where(lane == VEC * offset + row % VEC, summed, total)
    return jnp.sum(total, axis=0, keepdims=True)


def entry(gram, base, i, j):
    lane = base + VEC * ((j - i) % VEC) + i
    return gram[:, lane : lane + 1]


def assemble(entries):
    lane, row = iota((VEC, LANES), 1), iota((VEC, LANES), 0)
    total = jnp.zeros((VEC, LANES), jnp.float32)
    for (i, j), value in entries.items():
        total = jnp.where((row == i) & (lane == j), value, total)
    return total


def factorize(gram, base):
    a = {(i, j): entry(gram, base, i, j) * (1.0 / ORDER) for i in range(VEC) for j in range(i + 1)}
    low, inv = {}, {}
    for j in range(VEC):
        pivot = a[j, j] + epsilon
        for k in range(j):
            pivot = pivot - low[j, k] * low[j, k]
        low[j, j] = jnp.sqrt(pivot)
        inv[j, j] = 1.0 / low[j, j]
        for i in range(j + 1, VEC):
            rest = a[i, j]
            for k in range(j):
                rest = rest - low[i, k] * low[j, k]
            low[i, j] = rest * inv[j, j]
    for j in range(VEC):
        for i in range(j + 1, VEC):
            rest = low[i, j] * inv[j, j]
            for k in range(j + 1, i):
                rest = rest + low[i, k] * inv[k, j]
            inv[i, j] = -rest * inv[i, i]
    flip = lambda entries: {(j, i): value for (i, j), value in entries.items()}
    return assemble(low), assemble(inv), assemble(flip(inv)), assemble(flip(low))


def projected(gram, inverse, inverse_t):
    entries = {}
    for i in range(VEC):
        for j in range(i + 1):
            value = (entry(gram, 0, i, j) + entry(gram, 0, j, i)) * (1.0 / ORDER)
            entries[i, j] = value
            entries[j, i] = value
    return apply(apply(inverse, assemble(entries)), inverse_t)


def split(block, row):
    high = block.astype(jnp.bfloat16).astype(jnp.float32)
    return jnp.where(row < VEC, high, block - high)


def twice(block):
    return jnp.concatenate([block, block], axis=0)


def kernel(
    x_hbm, tiles_hbm, rows_hbm, cols_hbm, count_hbm,
    basis_ref, resid_ref, coef_ref,
    x_ref, rows_ref, cols_ref, count_ref, raw, t_high, t_low, own, xr, xc, row_parts, col_parts, col_packed,
    fp, bp, fr, br, fm, bm, gsrc, gy, gp, isem, tsem, ssem, rsem,
):
    r, c = lax.axis_index("row"), lax.axis_index("col")
    y, core, z, x = lax.div(r, 2), lax.rem(r, 2), lax.div(c, 4), lax.rem(c, 4)
    group = 2 * r + lax.div(c, HALF)
    owner_row, owner_col = lax.div(c, 2), HALF * lax.rem(c, 2)
    lane_at = lax.rem(c, HALF)
    eight = iota((8, LANES), 0)

    turn = lax.rem(x + 4 - 2 * core, 4)
    keeper = turn < 2
    odd = lax.rem(turn, 2)
    kept_part = lax.rem(z + 8 - y, 8)
    kept_group = 2 * r + odd

    def send(src, dst, exchange, row, col):
        pltpu.make_async_remote_copy(
            src_ref=src, dst_ref=dst, send_sem=ssem.at[exchange], recv_sem=rsem.at[exchange],
            device_id=(row, col), device_id_type=MESH,
        ).start()

    def send_or_keep(src, dst, exchange, row, col):
        mine = (row == r) & (col == c)

        @pl.when(mine)
        def _():
            pltpu.make_async_copy(src, dst, rsem.at[exchange]).start()

        @pl.when(jnp.logical_not(mine))
        def _():
            send(src, dst, exchange, row, col)

    def wait(sem, ref):
        pltpu.make_async_copy(ref, ref, sem).wait()

    def loop(first, last, body):
        def step(j, carry):
            body(j)
            return carry
        lax.fori_loop(first, last, step, 0)

    def outward(size):
        return [size // 2 + (j + 1) // 2 * (1 - 2 * (j % 2)) for j in range(size)]

    plane_z = [4 * lax.rem(z + away, 8) for away in outward(8)]
    plane_x = [lax.rem(x + away, 4) for away in outward(4)]
    line_y = [2 * lax.rem(y + away, 8) for away in outward(8)]
    line_core = [1 - core, core]

    def over_plane(body):
        for at in range(COLS - 1):
            body(plane_z[at // 4] + plane_x[at % 4])

    def over_line(body, count=ROWS - 1):
        for at in range(count):
            body(line_y[at // 2] + line_core[at % 2])

    pending = []

    pltpu.make_async_copy(x_hbm, x_ref, isem.at[0]).start()
    barrier = pltpu.get_barrier_semaphore()

    def greet(row, col):
        pl.semaphore_signal(barrier, 1, device_id=(row, col), device_id_type=MESH)


    @pl.when(owner_row != r)
    def _():
        for j in range(HALF):
            greet(owner_row, owner_col + j)

    over_line(lambda row: greet(row, group))
    over_plane(lambda col: greet(r, col))
    for k in range(SLOTS):
        pltpu.make_async_copy(tiles_hbm.at[k], raw.at[k], tsem.at[k]).start()
    pltpu.make_async_copy(rows_hbm, rows_ref, isem.at[1]).start()
    pltpu.make_async_copy(cols_hbm, cols_ref, isem.at[2]).start()
    pltpu.make_async_copy(count_hbm, count_ref, isem.at[3]).start()
    wait(isem.at[0], x_ref)
    pl.semaphore_wait(barrier, jnp.where(owner_row != r, COLS - 1 + ROWS - 1 + HALF, COLS - 1 + ROWS - 1))

    def line_start(at, value, exchange):
        gsrc[2 * at] = value
        gy[at, r] = value
        over_line(lambda row: send(gsrc.at[2 * at], gy.at[at, r], exchange, row, c))
        pending.append((exchange, gy.at[at, pl.ds(0, ROWS - 1)], None))

    def plane_start(at, line_exchange, exchange):
        wait(rsem.at[line_exchange], gy.at[at, pl.ds(0, ROWS - 1)])
        value = jnp.sum(gy[at], axis=0)
        gsrc[2 * at + 1] = value
        gp[at, c] = value
        over_plane(lambda col: send(gsrc.at[2 * at + 1], gp.at[at, c], exchange, r, col))
        pending.append((exchange, gp.at[at, pl.ds(0, COLS - 1)], None))

    def plane_done(at, exchange):
        wait(rsem.at[exchange], gp.at[at, pl.ds(0, COLS - 1)])
        return jnp.sum(gp[at], axis=0)

    def spread(step, values, places, out, tiles):
        for t in range(tiles):
            total = jnp.where(places[0] == t, values[0], 0.0)
            for k in range(1, SLOTS):
                total = total + jnp.where(places[k] == t, values[k], 0.0)
            out[step, 2 * t] = total[:VEC]
            out[step, 2 * t + 1] = total[VEC:]

    def places():
        row_at = [lax.rem(rows_ref[k], ROW_TILES) for k in range(SLOTS)]
        col_at = [lax.rem(cols_ref[k], COL_TILES) for k in range(SLOTS)]
        masks = [jnp.where(k < count_ref[0], 1.0, 0.0).astype(jnp.float32) for k in range(SLOTS)]
        return row_at, col_at, masks

    def multiply(k, parts, at, dims, mask):
        block = parts[pl.ds(2 * at, 2)]
        block = jnp.concatenate([block[0], block[1]], axis=1).astype(jnp.bfloat16)
        high = lax.dot_general(block, t_high[k], (dims, ((), ())), preferred_element_type=jnp.float32)
        low = lax.dot_general(block, t_low[k], (dims, ((), ())), preferred_element_type=jnp.float32)
        both = high + low
        left, right = both[:, :LANES], both[:, LANES:]
        left = left + pltpu.roll(left, VEC, 0)
        right = right + pltpu.roll(right, VEC, 0)
        return jnp.where(eight < VEC, left, right) * mask

    def crossed(backward, col_at):
        cross = [jnp.zeros((8, LANES), jnp.float32) for _ in range(VEC)]
        for k in range(SLOTS):
            entries = col_packed[col_at[k]]
            for offset in range(VEC):
                cross[offset] = cross[offset] + entries * rotated(backward[k], offset)
        return gram_row(cross)

    def own_gram(block):
        block = twice(block)
        half = jnp.where(eight < VEC, block, 0.0)
        return gram_row([half * rotated(block, offset) for offset in range(VEC)])

    dst = xc.at[0, lane_at]
    over_line(lambda row: send(x_ref, dst, COL0, row, group))
    send_or_keep(x_ref, dst, COL0, r, group)
    over_plane(lambda col: send(x_ref, xr.at[0, c], ROW0, r, col))
    start = x_ref[...]
    xr[0, c] = start
    pending.append((ROW0, xr.at[0, pl.ds(0, COLS - 1)], None))
    pending.append((COL0, xc.at[0, pl.ds(0, ROWS - 1)], None))
    pending.append((COL0, xc.at[0, 0], group != c))

    def halve(k):
        wait(tsem.at[k], raw.at[k])
        tile = raw[k]
        high = tile.astype(jnp.bfloat16)
        t_high[k] = high
        t_low[k] = (tile - high.astype(jnp.float32)).astype(jnp.bfloat16)

    loop(0, SLOTS, halve)
    wait(isem.at[1], rows_ref)
    wait(isem.at[2], cols_ref)
    wait(isem.at[3], count_ref)
    row_at, col_at, masks = places()
    start_row = pltpu.roll(own_gram(start), 16, 1)
    wait(rsem.at[ROW0], xr.at[0, pl.ds(0, COLS - 1)])
    for t in range(COLS):
        row_parts[t] = split(twice(xr[0, t]), eight)
    backward = [multiply(k, row_parts, row_at[k], ((1,), (0,)), masks[k]) for k in range(SLOTS)]
    spread(0, backward, col_at, bp, COL_TILES)

    for at, q in enumerate(outward(8)):
        send_or_keep(bp.at[0, pl.ds(KEPT * q, KEPT)], bm.at[r], BWD0, owner_row, plane_z[at] + x)
    wait(rsem.at[COL0], xc.at[0])
    for t in range(COL_TILES):
        left, right = twice(xc[0, 2 * t]), twice(xc[0, 2 * t + 1])
        col_parts[2 * t] = split(left, eight)
        col_parts[2 * t + 1] = split(right, eight)
        col_packed[t] = jnp.where(eight < VEC, left, right)
    forward = [multiply(k, col_parts, col_at[k], ((1,), (1,)), masks[k]) for k in range(SLOTS)]
    spread(0, forward, row_at, fp, ROW_TILES)
    for at, away in enumerate(outward(8)):
        q = lax.rem(z + 8 - y + away, 8)
        for half in range(2):
            part = fp.at[0, pl.ds(HALF * half + KEPT * q, KEPT)]
            send_or_keep(part, fm.at[c], FWD0, r, plane_z[at] + 2 * core + half)
    line_start(0, crossed(backward, col_at) + start_row, LINE0)
    pending.append((BWD0, bp.at[0, pl.ds(0, HALF - KEPT)], None))
    pending.append((BWD0, bp.at[0, pl.ds(0, KEPT)], jnp.logical_not(keeper & (kept_group == c))))
    pending.append((FWD0, fp.at[0, pl.ds(0, COLS - KEPT)], None))
    pending.append((FWD0, fp.at[0, pl.ds(0, KEPT)], jnp.logical_not(keeper)))
    plane_start(0, LINE0, PLANE0)

    kept_at = HALF * odd + KEPT * kept_part
    at_row = xr.at[1, pl.ds(kept_at, KEPT)]
    at_col = xc.at[1, pl.ds(KEPT * kept_part, KEPT)]

    @pl.when(keeper)
    def _():
        wait(rsem.at[FWD0], fm)
        total = jnp.sum(fm[...], axis=0)
        wait(rsem.at[BWD0], bm)
        own[...] = total + jnp.sum(bm[...], axis=0)
        over_plane(lambda col: send(own, at_row, ROW1, r, col))
        over_line(lambda row: send_or_keep(own, at_col, COL1, row, kept_group), ROWS)
        pltpu.make_async_copy(own, at_row, rsem.at[ROW1]).start()

    for lap in range(KEPT):
        pending.append((ROW1, xr.at[1, pl.ds(0, COLS - 1)], keeper))
        pending.append((COL1, xc.at[1, pl.ds(0, ROWS - 1)], keeper))
    pending.append((COL1, xc.at[1, pl.ds(0, KEPT)], keeper & (kept_group != c)))

    gram = plane_done(0, PLANE0)
    _, inverse, inverse_t, _ = factorize(gram, 16)
    first_diag = projected(gram, inverse, inverse_t)
    first_basis = apply(inverse, start)
    from_start = -apply(first_diag, inverse)
    inverse_twice, start_factor_twice = twice(inverse), twice(from_start)
    of_image = [jnp.broadcast_to(inverse_twice[:, j : j + 1], (8, LANES)) for j in range(VEC)]
    of_start = [jnp.broadcast_to(start_factor_twice[:, j : j + 1], (8, LANES)) for j in range(VEC)]

    def combined(ref, at):
        total = of_image[0] * ref[1, at, 0:1, :] + of_start[0] * ref[0, at, 0:1, :]
        for j in range(1, VEC):
            total = total + (of_image[j] * ref[1, at, j : j + 1, :] + of_start[j] * ref[0, at, j : j + 1, :])
        return total

    kept = [apply(inverse, own[at]) + apply(from_start, xr[0, kept_at + at]) for at in range(KEPT)]
    rest_row = sum(own_gram(block) for block in kept)
    line_start(1, jnp.where(keeper, rest_row, 0.0), LINE1)
    wait(rsem.at[ROW1], xr.at[1])
    for t in range(COLS):
        row_parts[t] = split(combined(xr, t), eight)
    backward = [multiply(k, row_parts, row_at[k], ((1,), (0,)), masks[k]) for k in range(SLOTS)]
    spread(1, backward, col_at, bp, COL_TILES)

    def back(j):
        s = lax.rem(c + j, HALF)
        send_or_keep(bp.at[1, s], br.at[r], BWD1, owner_row, owner_col + s)

    wait(rsem.at[COL1], xc.at[1])
    for t in range(COL_TILES):
        left, right = combined(xc, 2 * t), combined(xc, 2 * t + 1)
        col_parts[2 * t] = split(left, eight)
        col_parts[2 * t + 1] = split(right, eight)
        col_packed[t] = jnp.where(eight < VEC, left, right)
    line_start(2, crossed(backward, col_at), LINE2)
    for j in range(HALF):
        back(j)
    forward = [multiply(k, col_parts, col_at[k], ((1,), (1,)), masks[k]) for k in range(SLOTS)]
    spread(1, forward, row_at, fp, ROW_TILES)
    over_plane(lambda col: send(fp.at[1, col], fr.at[c], FWD1, r, col))
    fr[c] = fp[1, c]
    pending.append((FWD1, fr.at[pl.ds(0, COLS - 1)], None))
    pending.append((BWD1, br.at[pl.ds(0, HALF - 1)], None))
    pending.append((BWD1, br.at[0], group != c))
    plane_start(1, LINE1, PLANE1)
    plane_start(2, LINE2, PLANE2)
    gram = plane_done(1, PLANE1)
    rest = apply(inverse, xr[1, c]) + apply(from_start, start)
    factor, inverse, inverse_t, factor_t = factorize(gram, 0)
    next_basis = apply(inverse, rest)
    basis_ref[...] = next_basis
    wait(rsem.at[FWD1], fr.at[pl.ds(0, COLS - 1)])
    image = jnp.sum(fr[...], axis=0)
    wait(rsem.at[BWD1], br)
    image = image + jnp.sum(br[...], axis=0)
    known = apply(inverse, image) - apply(factor_t, first_basis)
    for exchange, ref, condition in pending[:-1]:
        if condition is None:
            wait(ssem.at[exchange], ref)
        else:
            pl.when(condition)(lambda exchange=exchange, ref=ref: wait(ssem.at[exchange], ref))
    gram = plane_done(2, PLANE2)
    second_diag = projected(gram, inverse, inverse_t)
    resid_ref[...] = known - apply(second_diag, next_basis)
    coef_ref[0] = first_diag[:, :VEC]
    coef_ref[1] = second_diag[:, :VEC]
    coef_ref[2] = factor[:, :VEC]
    wait(ssem.at[pending[-1][0]], pending[-1][1])


def settle(basis, resid, coef, basis_out, resid_out, coef_out, sem):
    copies = [
        pltpu.make_async_copy(src, dst, sem.at[at])
        for at, (src, dst) in enumerate(((basis, basis_out), (resid, resid_out), (coef, coef_out)))
    ]
    for copy in copies:
        copy.start()
    for copy in copies:
        copy.wait()


def body(start_block, matrix_tiles, tile_rows, tile_cols, tile_counts):
    share = jax.ShapeDtypeStruct((VEC, LANES), jnp.float32)
    shapes = (share, share, jax.ShapeDtypeStruct((3, VEC, VEC), jnp.float32))
    vmem, anywhere = pl.BlockSpec(memory_space=pltpu.VMEM), pl.BlockSpec(memory_space=pl.ANY)
    buffer = lambda *shape: pltpu.VMEM(shape, jnp.float32)
    found = pl.pallas_call(
        kernel,
        out_shape=tuple(pltpu.VMEM(shape.shape, shape.dtype) for shape in shapes),
        in_specs=[anywhere] * 5,
        out_specs=(vmem, vmem, vmem),
        scratch_shapes=[
            buffer(VEC, LANES),
            pltpu.SMEM((SLOTS,), jnp.int32),
            pltpu.SMEM((SLOTS,), jnp.int32),
            pltpu.SMEM((1,), jnp.int32),
            buffer(SLOTS, TILE, TILE),
            pltpu.VMEM((SLOTS, TILE, TILE), jnp.bfloat16),
            pltpu.VMEM((SLOTS, TILE, TILE), jnp.bfloat16),
            buffer(KEPT, VEC, LANES),
            buffer(2, COLS, VEC, LANES),
            buffer(2, HALF, VEC, LANES),
            buffer(COLS, 8, LANES),
            buffer(HALF, 8, LANES),
            buffer(COL_TILES, 8, LANES),
            buffer(2, COLS, VEC, LANES),
            buffer(2, HALF, VEC, LANES),
            buffer(COLS, VEC, LANES),
            buffer(ROWS, VEC, LANES),
            buffer(COLS, KEPT, VEC, LANES),
            buffer(ROWS, KEPT, VEC, LANES),
            buffer(6, 1, LANES),
            buffer(3, ROWS, 1, LANES),
            buffer(3, COLS, 1, LANES),
            pltpu.SemaphoreType.DMA((4,)),
            pltpu.SemaphoreType.DMA((SLOTS,)),
            pltpu.SemaphoreType.DMA((14,)),
            pltpu.SemaphoreType.DMA((14,)),
        ],
        compiler_params=pltpu.CompilerParams(collective_id=0, has_side_effects=True),
    )(start_block, matrix_tiles, tile_rows, tile_cols, tile_counts)
    return pl.pallas_call(
        settle,
        out_shape=shapes,
        in_specs=[vmem] * 3,
        out_specs=(anywhere, anywhere, anywhere),
        scratch_shapes=[pltpu.SemaphoreType.DMA((3,))],
    )(*[pltpu.with_memory_space_constraint(f, pltpu.VMEM) for f in found])


def solution(mesh):
    return jax.shard_map(
        body,
        mesh=mesh,
        in_specs=(
            P(None, ("row", "col")),
            P(("row", "col"), None, None),
            P(("row", "col")),
            P(("row", "col")),
            P(("row", "col")),
        ),
        out_specs=(P(None, ("row", "col")), P(None, ("row", "col")), P()),
        check_vma=False,
    )
```
